256 devices in a mesh: ctx: 64 (over z, y, core), ch: 4 (over x).
Axes of the slice: x: 4, y: 4, z: 8, core: 2. Of those that a mesh axis runs over, the one named last changes fastest.
Arguments:
- features: bfloat16 [12288, 4096], P('ctx', 'ch'), may hold values from -6 to 6
- w_in: bfloat16 [4096, 3, 2048], P('ctx', None, 'ch'), may hold values from -0.09375 to 0.09375
- short_filter: float32 [3, 3, 2048], P(None, None, 'ch'), may hold values from -3 to 3
- filter_spectrum: float32 [2, 12288, 2048], P(None, 'ctx', 'ch'), may hold values from -6 to 6
- out_grad: bfloat16 [12288, 4096], P('ctx'), may hold values from -0.15625 to 0.15625
Outputs:
- gated: bfloat16 [12288, 2048], P('ctx', 'ch')
- w_out_grad: float32 [4096, 2048], P('ctx', 'ch')
The draws below stay inside these ranges and needn't reach their ends.
All inputs are finite; a program needn't handle non-finite values.
Results may differ from the reference program's by a relative error of at most 0.0065.
Values may be sent and summed in bfloat16 or wider, within the bound.
A program may use at most 128 MiB of HBM per device.

```python
import jax
import jax.numpy as jnp

D = 4096
L_DEV = 192
SHARDS = 64
SECTIONS = 6
CHANNELS = 2048
TOKENS = 12288


def strengthened(drawn, stream_key, source, target, shards_of, factor):
    owner, partner = [(jnp.arange(drawn.shape[axis_at]) // (drawn.shape[axis_at] // shards_of)).reshape([-1 if axis == axis_at else 1 for axis in range(drawn.ndim)]) for axis_at in (source, target)]
    chosen = jax.random.permutation(stream_key, shards_of)[partner]
    strong = (owner == chosen) | (owner == (partner + shards_of // 2) % shards_of)
    return jnp.where(strong, factor * drawn, drawn)


def block_scale(own_key, shape, shards, low, high):
    def one(axis_at, parts):
        draws = jax.random.uniform(jax.random.fold_in(jax.random.fold_in(own_key, 6), axis_at), (parts,), jnp.float32, low / len(shards), high / len(shards))
        return jnp.repeat(jnp.exp(draws), shape[axis_at] // parts).reshape((-1,) + (1,) * (len(shape) - axis_at - 1))

    gain = one(*shards[0])
    for cut in shards[1:]:
        gain = gain * one(*cut)
    return gain


def scatter_about(rng, extent, spread, limit, pieces=(), kind=jnp.bfloat16):
    factor_of = block_scale(rng, extent, pieces, -0.22, 0.18) if pieces else 1.0
    entries = jax.random.normal(rng, extent, jnp.float32) * spread * factor_of
    return jnp.minimum(jnp.maximum(entries, -limit), limit).astype(kind)


def noise_with(own_key, extent, spread, most, split, heavy, kind=jnp.bfloat16):
    array = spread * jax.random.normal(own_key, extent, jnp.float32)
    if split:
        array = array * block_scale(own_key, extent, split, -0.22, 0.18)
    return jnp.clip(strengthened(array, jax.random.fold_in(own_key, 3), *heavy), -most, most).astype(kind)


def setup_inputs(seed: int = 0) -> dict:
    splits = jax.random.split(jax.random.key(seed), 6)
    return {
        "features": scatter_about(splits[0], (TOKENS, D), 1.0, 6.0, ((0, 64), (1, 4))),
        "w_in": scatter_about(splits[1], (D, 3, CHANNELS), D ** -0.5, 0.09375, ((0, 64), (2, 4))),
        "short_filter": scatter_about(splits[2], (3, 3, CHANNELS), 0.6, 3.0, ((2, 4),), jnp.float32),
        "filter_spectrum": scatter_about(splits[3], (2, TOKENS, CHANNELS), 1.0, 6.0, ((1, 64), (2, 4)), jnp.float32),
        "out_grad": noise_with(splits[4], (TOKENS, D), 0.01, 0.15625, ((0, 64),), (0, 1, 64, 4.0)),
    }


def reverse_bits(values, count):
    result = jnp.zeros_like(values)
    for level in range(count):
        result = result | (((values >> level) & 1) << (count - 1 - level))
    return result


def reference(features, w_in, short_filter, filter_spectrum, out_grad):
    projected = jnp.dot(features, w_in.reshape(D, 3 * CHANNELS), preferred_element_type=jnp.float32)
    projected = projected.astype(jnp.bfloat16).reshape(TOKENS, 3, CHANNELS)
    leading = jnp.zeros((2, 3, CHANNELS), jnp.bfloat16)
    extended = jnp.concatenate([leading, projected], axis=0).astype(jnp.float32)
    mixed = short_filter[0] * extended[2:] + short_filter[1] * extended[1:TOKENS + 1] + short_filter[2] * extended[:TOKENS]
    query = mixed[:, 0]
    signal = mixed[:, 1] * mixed[:, 2]
    frequency = jnp.arange(TOKENS, dtype=jnp.int32)
    source_rows = (reverse_bits(frequency % SHARDS, SECTIONS) * L_DEV + frequency // SHARDS).astype(jnp.int32)
    filter_real = jnp.take(filter_spectrum[0], source_rows, axis=0)
    filter_imag = jnp.take(filter_spectrum[1], source_rows, axis=0)
    spectrum = jnp.fft.fft(signal, axis=0)
    convolved = jnp.real(jnp.fft.ifft(spectrum * (filter_real + 1j * filter_imag), axis=0))
    gated = (query * convolved).astype(jnp.bfloat16)
    w_out_grad = jnp.dot(out_grad.T, gated, preferred_element_type=jnp.float32)
    return gated, w_out_grad
```

```python
import math

import jax
import jax.numpy as jnp
import numpy as np
from jax import lax
from jax.sharding import Mesh, PartitionSpec as P

CTX = ("z", "y", "core")
HIGH = lax.Precision.HIGHEST


def bit_reversed(count):
    bits = count.bit_length() - 1
    return np.array([int(format(i, f"0{bits}b")[::-1], 2) for i in range(count)])


def tables(shards, rows):
    total = shards * rows
    k1 = bit_reversed(shards)
    outer = 2 * np.pi / shards * np.outer(k1, np.arange(shards))
    turn = 2 * np.pi / total * np.outer(k1, np.arange(rows))
    inner = 2 * np.pi / rows * (np.outer(np.arange(rows), np.arange(rows)) % rows)
    f = lambda a: np.asarray(a, np.float32)
    return (
        f(np.concatenate([np.cos(outer), -np.sin(outer)])),
        f(np.cos(turn))[:, None, :],
        f(np.sin(turn))[:, None, :],
        f(np.block([[np.cos(inner), -np.sin(inner)], [np.sin(inner), np.cos(inner)]])),
    )


def on_device(features, w_in, short_filter, filter_spectrum, out_grad):
    rows = features.shape[0]
    width = w_in.shape[2]
    shards = lax.axis_size(CTX)
    zs = lax.axis_size("z")
    near = shards // zs
    total = rows * shards
    per = width // shards
    place = lax.axis_index(CTX)
    whole = lax.all_gather(features, "ch", axis=1, tiled=True)
    piece = lax.all_gather(w_in, CTX, axis=0, tiled=True)
    projected = jnp.dot(
        whole, piece.reshape(piece.shape[0], 3 * width), preferred_element_type=jnp.float32
    )
    projected = projected.astype(jnp.bfloat16).reshape(rows, 3, width)
    earlier = lax.ppermute(
        projected[rows - 2 :], CTX, [(i, i + 1) for i in range(shards - 1)]
    )
    extended = jnp.concatenate([earlier, projected], axis=0).astype(jnp.float32)
    mixed = (
        short_filter[0] * extended[2:]
        + short_filter[1] * extended[1 : rows + 1]
        + short_filter[2] * extended[:rows]
    )
    query = mixed[:, 0]
    signal = mixed[:, 1] * mixed[:, 2]

    outer, turn_cos, turn_sin, inner = tables(shards, rows)
    freq = filter_spectrum.astype(jnp.bfloat16).transpose(2, 0, 1).reshape(shards, per, 2, rows)
    freq = lax.all_to_all(freq, CTX, 0, 0, tiled=True).astype(jnp.float32)
    sent = signal.astype(jnp.bfloat16).T.reshape(shards, per * rows)
    data = lax.all_to_all(sent, CTX, 0, 0, tiled=True)
    data = jnp.dot(outer, data.astype(jnp.float32), precision=HIGH).reshape(2, shards, per, rows)
    turned = jnp.concatenate(
        [
            data[0] * turn_cos + data[1] * turn_sin,
            data[1] * turn_cos - data[0] * turn_sin,
        ],
        axis=-1,
    )
    spec = jnp.dot(turned, inner, precision=HIGH)
    spec_real, spec_imag = spec[..., :rows], spec[..., rows:]
    freq_real, freq_imag = freq[:, :, 0], freq[:, :, 1]
    prod = jnp.concatenate(
        [
            spec_real * freq_real - spec_imag * freq_imag,
            spec_real * freq_imag + spec_imag * freq_real,
        ],
        axis=-1,
    )
    back = lax.dot_general(prod, inner, (((2,), (1,)), ((), ())), precision=HIGH) / total
    back_real, back_imag = back[..., :rows], back[..., rows:]
    turned = jnp.concatenate(
        [
            back_real * turn_cos - back_imag * turn_sin,
            back_imag * turn_cos + back_real * turn_sin,
        ],
        axis=0,
    ).reshape(2 * shards, per * rows)
    convolved = jnp.dot(outer.T, turned, precision=HIGH).astype(jnp.bfloat16)
    convolved = lax.all_to_all(convolved, CTX, 0, 0, tiled=True)
    convolved = convolved.reshape(width, rows).T.astype(jnp.float32)
    gated = (query * convolved).astype(jnp.bfloat16)

    spread = out_grad.reshape(rows, zs, near, -1).transpose(2, 0, 1, 3).reshape(near, rows, -1)
    spread = lax.all_to_all(spread, ("y", "core"), 0, 0, tiled=True).reshape(near * rows, -1)
    column = lax.all_gather(gated, ("y", "core"), axis=0, tiled=True)
    w_out_grad = lax.psum_scatter(
        lax.dot_general(
            spread, column, (((0,), (0,)), ((), ())), preferred_element_type=jnp.float32
        ),
        "z",
        scatter_dimension=0,
        tiled=True,
    )
    return (gated, w_out_grad)


def solution(mesh):
    fine = Mesh(mesh.devices.reshape(8, 4, 2, 4), ("z", "y", "core", "ch"))
    in_specs = (
        P(CTX, "ch"),
        P(CTX, None, "ch"),
        P(None, None, "ch"),
        P(None, CTX, "ch"),
        P(CTX, None),
    )
    out_specs = (P(CTX, "ch"), P(CTX, "ch"))
    return jax.shard_map(
        on_device, mesh=fine, in_specs=in_specs, out_specs=out_specs, check_vma=False
    )
```

```python
import functools
import heapq

import jax
import jax.numpy as jnp
import numpy as np
from jax import lax
from jax.experimental import pallas as pl
from jax.experimental.pallas import tpu as pltpu
from jax.sharding import Mesh, PartitionSpec as P

CTX = ("z", "y", "core")
MESH = pl.DeviceIdType.MESH
HALO = 16
TILE = 256
MATMUL_FROM = 36
HIGH = lax.Precision.HIGHEST


def bit_reversed(count):
    bits = count.bit_length() - 1
    return np.array([int(format(i, f"0{bits}b")[::-1], 2) for i in range(count)])


def tables(shards, rows):
    total = shards * rows
    k1 = bit_reversed(shards)
    outer = 2 * np.pi / shards * np.outer(k1, np.arange(shards))
    turn = 2 * np.pi / total * np.outer(k1, np.arange(rows))
    inner = 2 * np.pi / rows * (np.outer(np.arange(rows), np.arange(rows)) % rows)
    f = lambda a: np.asarray(a, np.float32)
    return (
        f(np.concatenate([np.cos(outer), -np.sin(outer)])),
        f(np.cos(turn))[:, None, :],
        f(np.sin(turn))[:, None, :],
        f(np.block([[np.cos(inner), -np.sin(inner)], [np.sin(inner), np.cos(inner)]])),
    )


def ring_plan(zs, ys, share):
    z_max, z_min = zs // 2, -((zs - 1) // 2)
    y_max, y_min = ys // 2, -((ys - 1) // 2)
    size = {0: share * 2.1, 1: (1 - share) * 2.1}

    def steps(at, low, high):
        if at == 0:
            return [d for d, ok in ((1, high > 0), (-1, low < 0)) if ok]
        return [1] if 0 < at < high else [-1] if low < at < 0 else []

    def onward(part, fz, fy):
        along_z = [("z", d, (fz + d, fy)) for d in steps(fz, z_min, z_max)]
        along_y = [("y", d, (fz, fy + d)) for d in steps(fy, y_min, y_max)]
        if part == 0:
            return (along_y if fz == 0 else []) + along_z
        return (along_z if fy == 0 else []) + along_y

    free = {"y": 0.0, "z": 0.0}
    order, count = [], 2
    waiting = [(0.0, 0, 1, 0, 0), (0.0, 1, 0, 0, 0)]
    while waiting:
        now, _, part, fz, fy = heapq.heappop(waiting)
        sends = onward(part, fz, fy)
        order.append((part, fz, fy, sends))
        for axis, _, key in sends:
            free[axis] = max(free[axis], now) + size[part]
            count += 1
            heapq.heappush(waiting, (free[axis] + 1.7, count, part, *key))
    return order


def project_kernel(
    sizes, x_in, w_in, taps, query, signal, x_all, w_all, total,
    local_sem, ring_send, ring_recv, twin_send, twin_recv, x_send, x_recv,
    halo_send, halo_recv, edge_send, edge_recv,
):
    zs, ys, xs = sizes
    rows, depth = x_in.shape
    piece, flat = w_in.shape
    width = flat // 3
    first = 5 * flat // 12 // 128 * 128
    z, y, core, x = (lax.axis_index(a) for a in ("z", "y", "core", "ch"))
    turn = 1 - 2 * core
    wrap = lambda v, n: lax.rem(v + 2 * n, n)
    here = (z * ys + y) * 2 + core
    shards = zs * ys * 2
    after, before = lax.rem(here + 1, shards), lax.rem(here + shards - 1, shards)

    def device(place):
        return {"z": place // (2 * ys), "y": place // 2 % ys, "core": place % 2, "ch": x}

    def by_axis(axis, step):
        if axis == "z":
            return {"z": wrap(z + turn * step, zs), "y": y, "core": core, "ch": x}
        if axis == "y":
            return {"z": z, "y": wrap(y + turn * step, ys), "core": core, "ch": x}
        return {"z": z, "y": y, "core": core, "ch": lax.rem(x + step, xs)}

    twin = {"z": z, "y": y, "core": 1 - core, "ch": x}
    peers = [by_axis("z", 1), by_axis("z", -1), by_axis("y", 1), by_axis("y", -1), twin]
    peers += [by_axis("ch", d) for d in range(1, xs)] + [device(after), device(before)]
    barrier = pltpu.get_barrier_semaphore()
    for peer in peers:
        pl.semaphore_signal(barrier, inc=1, device_id=peer, device_id_type=MESH)
    pl.semaphore_wait(barrier, len(peers))

    def remote(src, dst, send, recv, to):
        return pltpu.make_async_remote_copy(
            src_ref=src, dst_ref=dst, send_sem=send, recv_sem=recv,
            device_id=to, device_id_type=MESH,
        )

    sends = []

    def start(copy):
        copy.start()
        sends.append(copy)

    z_low, y_low = (zs - 1) // 2, (ys - 1) // 2
    columns = (slice(0, first), slice(first, flat))

    def slot(fz, fy, sign=1, of_core=None):
        zo, yo = wrap(z - sign * turn * fz, zs), wrap(y - sign * turn * fy, ys)
        which = (zo * ys + yo) * 2 + (core if of_core is None else of_core)
        return pl.ds(pl.multiple_of(which * piece, piece), piece)

    def ring_copy(part, origin, key, axis, step):
        where = slot(*origin)
        src = w_in.at[:, columns[part]] if origin == (0, 0) else w_all.at[where, columns[part]]
        sem = (part, key[0] + z_low, key[1] + y_low)
        return remote(
            src, w_all.at[where, columns[part]], ring_send.at[sem], ring_recv.at[sem],
            by_axis(axis, step),
        )

    def x_rows(of, n, row):
        return x_all.at[pl.ds(row, n), pl.ds(pl.multiple_of(of * depth, depth), depth)]

    plan = ring_plan(zs, ys, first / flat)
    own_w = pltpu.make_async_copy(w_in, w_all.at[slot(0, 0)], local_sem.at[0])
    own_x = pltpu.make_async_copy(x_in, x_rows(x, rows, HALO), local_sem.at[1])
    start(remote(x_in.at[pl.ds(rows - HALO, HALO)], x_rows(x, HALO, 0), edge_send, edge_recv, device(after)))
    arrived = set()
    x_done = False
    pending = []

    def wait_x():
        own_x.wait()
        edge = remote(x_in.at[pl.ds(0, HALO)], x_rows(x, HALO, 0), edge_send, edge_recv, device(after))
        edge.wait_recv()
        for d in range(1, xs):
            start(remote(x_rows(x, HALO, 0), x_rows(x, HALO, 0), halo_send.at[d - 1], halo_recv.at[d - 1], by_axis("ch", d)))

    def wait_rest_of_x():
        for d in range(1, xs):
            of = lax.rem(x + xs - d, xs)
            remote(x_in, x_rows(of, rows, HALO), x_send.at[d - 1], x_recv.at[d - 1], by_axis("ch", d)).wait_recv()
        for d in range(1, xs):
            of = lax.rem(x + xs - d, xs)
            remote(x_rows(of, HALO, 0), x_rows(of, HALO, 0), halo_send.at[d - 1], halo_recv.at[d - 1], by_axis("ch", d)).wait_recv()

    span = 2 * ys * piece

    def mirror(f, n):
        return f if 2 * f == n else -f

    def multiply(fz, opening):
        for fy in range(-y_low, ys // 2 + 1):
            theirs = (mirror(fz, zs), mirror(fy, ys))
            sem = (theirs[0] + z_low, theirs[1] + y_low)
            where = slot(fz, fy, 1, 1 - core)
            remote(w_all.at[where], w_all.at[where], twin_send.at[sem], twin_recv.at[sem], twin).wait_recv()
        base = pl.multiple_of(wrap(z - turn * fz, zs) * span, span)
        left = x_all[:, pl.ds(base, span)]

        @pl.loop(0, flat // TILE)
        def _(tile):
            cols = pl.ds(pl.multiple_of(tile * TILE, TILE), TILE)
            part = jnp.dot(left, w_all[pl.ds(base, span), cols], preferred_element_type=jnp.float32)
            if opening:
                total[:, cols] = part
            else:
                total[:, cols] += part

    multiplied = []
    for index, (part, fz, fy, onward) in enumerate(plan):
        if (fz, fy) != (0, 0):
            sem = (part, fz + z_low, fy + y_low)
            where = slot(fz, fy)
            remote(
                w_all.at[where, columns[part]], w_all.at[where, columns[part]],
                ring_send.at[sem], ring_recv.at[sem], twin,
            ).wait_recv()
        for axis, step, key in onward:
            start(ring_copy(part, (fz, fy), key, axis, step))
        arrived.add((part, fz, fy))
        if (1 - part, fz, fy) in arrived:
            sem = (fz + z_low, fy + y_low)
            where = slot(fz, fy)
            src = w_in if (fz, fy) == (0, 0) else w_all.at[where]
            start(remote(src, w_all.at[where], twin_send.at[sem], twin_recv.at[sem], twin))
        if index == 1:
            own_w.start()
            own_x.start()
            for d in range(1, xs):
                start(remote(x_in, x_rows(x, rows, HALO), x_send.at[d - 1], x_recv.at[d - 1], by_axis("ch", d)))
        if index == 5:
            wait_x()
        ready = [k for k in range(-z_low, zs // 2 + 1) if k not in multiplied and k not in pending
                 and all((p, g, f) in arrived for p in (0, 1) for g in (k, mirror(k, zs)) for f in range(-y_low, ys // 2 + 1))]
        pending += sorted(ready, key=abs)
        if pending and index >= MATMUL_FROM and index % 3 == 0:
            if not multiplied:
                own_w.wait()
                wait_rest_of_x()
            fz_now = pending.pop(0)
            multiply(fz_now, not multiplied)
            multiplied.append(fz_now)
    for fz in pending:
        multiply(fz, not multiplied)
        multiplied.append(fz)
    assert sorted(multiplied) == list(range(-z_low, zs // 2 + 1))

    total[0:HALO] = jnp.where(here == 0, 0.0, total[0:HALO])
    for at in range(0, width, TILE):
        mixed = []
        for j in range(3):
            cols = slice(j * width + at, j * width + at + TILE)
            mixed.append(sum(
                taps[i : i + 1, cols]
                * total[HALO - i : HALO - i + rows, cols].astype(jnp.bfloat16).astype(jnp.float32)
                for i in range(3)
            ))
        query[:, at : at + TILE] = mixed[0]
        signal[:, at : at + TILE] = (mixed[1] * mixed[2]).astype(jnp.bfloat16)
    for copy in sends:
        copy.wait_send()


def project(features, w_in, short_filter, sizes):
    zs, ys, xs = sizes
    rows, depth = features.shape
    piece, _, width = w_in.shape
    flat = 3 * width
    dma = pltpu.SemaphoreType.DMA
    vmem = pl.BlockSpec(memory_space=pltpu.VMEM)
    return pl.pallas_call(
        functools.partial(project_kernel, sizes),
        out_shape=(
            jax.ShapeDtypeStruct((rows, width), jnp.float32),
            jax.ShapeDtypeStruct((rows, width), jnp.bfloat16),
        ),
        in_specs=[vmem] * 3,
        out_specs=(vmem, vmem),
        scratch_shapes=[
            pltpu.VMEM((rows + HALO, depth * xs), jnp.bfloat16),
            pltpu.VMEM((piece * zs * ys * 2, flat), jnp.bfloat16),
            pltpu.VMEM((rows + HALO, flat), jnp.float32),
            dma((2,)), dma((2, zs, ys)), dma((2, zs, ys)), dma((zs, ys)), dma((zs, ys)),
            dma((xs - 1,)), dma((xs - 1,)), dma((xs - 1,)), dma((xs - 1,)), dma, dma,
        ],
        compiler_params=pltpu.CompilerParams(
            collective_id=0, has_side_effects=True, vmem_limit_bytes=48 << 20
        ),
        name="project",
    )(features, w_in.reshape(piece, flat), short_filter.reshape(3, flat))


def on_device(features, w_in, short_filter, filter_spectrum, out_grad):
    rows = features.shape[0]
    width = w_in.shape[2]
    shards = lax.axis_size(CTX)
    zs = lax.axis_size("z")
    near = shards // zs
    total = rows * shards
    per = width // shards
    sizes = tuple(lax.axis_size(a) for a in ("z", "y", "ch"))
    query, signal = project(features, w_in, short_filter, sizes)

    outer, turn_cos, turn_sin, inner = tables(shards, rows)
    freq = filter_spectrum.astype(jnp.bfloat16).transpose(2, 0, 1).reshape(shards, per, 2, rows)
    freq = lax.all_to_all(freq, CTX, 0, 0, tiled=True).astype(jnp.float32)
    sent = signal.T.reshape(shards, per * rows)
    data = lax.all_to_all(sent, CTX, 0, 0, tiled=True)
    data = jnp.dot(outer, data.astype(jnp.float32), precision=HIGH).reshape(2, shards, per, rows)
    turned = jnp.concatenate(
        [
            data[0] * turn_cos + data[1] * turn_sin,
            data[1] * turn_cos - data[0] * turn_sin,
        ],
        axis=-1,
    )
    spec = jnp.dot(turned, inner, precision=HIGH)
    spec_real, spec_imag = spec[..., :rows], spec[..., rows:]
    freq_real, freq_imag = freq[:, :, 0], freq[:, :, 1]
    prod = jnp.concatenate(
        [
            spec_real * freq_real - spec_imag * freq_imag,
            spec_real * freq_imag + spec_imag * freq_real,
        ],
        axis=-1,
    )
    back = lax.dot_general(prod, inner, (((2,), (1,)), ((), ())), precision=HIGH) / total
    back_real, back_imag = back[..., :rows], back[..., rows:]
    turned = jnp.concatenate(
        [
            back_real * turn_cos - back_imag * turn_sin,
            back_imag * turn_cos + back_real * turn_sin,
        ],
        axis=0,
    ).reshape(2 * shards, per * rows)
    convolved = jnp.dot(outer.T, turned, precision=HIGH).astype(jnp.bfloat16)
    convolved = lax.all_to_all(convolved, CTX, 0, 0, tiled=True)
    convolved = convolved.reshape(width, rows).T.astype(jnp.float32)
    gated = (query * convolved).astype(jnp.bfloat16)

    spread = out_grad.reshape(rows, zs, near, -1).transpose(2, 0, 1, 3).reshape(near, rows, -1)
    spread = lax.all_to_all(spread, ("y", "core"), 0, 0, tiled=True).reshape(near * rows, -1)
    column = lax.all_gather(gated, ("y", "core"), axis=0, tiled=True)
    w_out_grad = lax.psum_scatter(
        lax.dot_general(
            spread, column, (((0,), (0,)), ((), ())), preferred_element_type=jnp.float32
        ),
        "z",
        scatter_dimension=0,
        tiled=True,
    )
    return (gated, w_out_grad)


def solution(mesh):
    fine = Mesh(mesh.devices.reshape(8, 4, 2, 4), ("z", "y", "core", "ch"))
    in_specs = (
        P(CTX, "ch"),
        P(CTX, None, "ch"),
        P(None, None, "ch"),
        P(None, CTX, "ch"),
        P(CTX, None),
    )
    out_specs = (P(CTX, "ch"), P(CTX, "ch"))
    return jax.shard_map(
        on_device, mesh=fine, in_specs=in_specs, out_specs=out_specs, check_vma=False
    )
```

```python
import functools
import heapq

import jax
import jax.numpy as jnp
import numpy as np
from jax import lax
from jax.experimental import pallas as pl
from jax.experimental.pallas import tpu as pltpu
from jax.sharding import Mesh, PartitionSpec as P

CTX = ("z", "y", "core")
MESH = pl.DeviceIdType.MESH
HALO = 16
TILE = 256
MATMUL_FROM = 36
F32 = jnp.float32
BF16 = jnp.bfloat16
HIGH = lax.Precision.HIGHEST


def ring_plan(zs, ys, share):
    z_max, z_min = zs // 2, -((zs - 1) // 2)
    y_max, y_min = ys // 2, -((ys - 1) // 2)
    size = {0: share * 2.1, 1: (1 - share) * 2.1}

    def steps(at, low, high):
        if at == 0:
            return [d for d, ok in ((1, high > 0), (-1, low < 0)) if ok]
        return [1] if 0 < at < high else [-1] if low < at < 0 else []

    def onward(part, fz, fy):
        along_z = [("z", d, (fz + d, fy)) for d in steps(fz, z_min, z_max)]
        along_y = [("y", d, (fz, fy + d)) for d in steps(fy, y_min, y_max)]
        if part == 0:
            return (along_y if fz == 0 else []) + along_z
        return (along_z if fy == 0 else []) + along_y

    free = {"y": 0.0, "z": 0.0}
    order, count = [], 2
    waiting = [(0.0, 0, 1, 0, 0), (0.0, 1, 0, 0, 0)]
    while waiting:
        now, _, part, fz, fy = heapq.heappop(waiting)
        sends = onward(part, fz, fy)
        order.append((part, fz, fy, sends))
        for axis, _, key in sends:
            free[axis] = max(free[axis], now) + size[part]
            count += 1
            heapq.heappush(waiting, (free[axis] + 1.7, count, part, *key))
    return order


def bit_reversed(count):
    bits = count.bit_length() - 1
    return np.array([int(format(i, f"0{bits}b")[::-1], 2) for i in range(count)])


def halves(table):
    high = table.astype(BF16)
    return high, (table - high.astype(np.float64)).astype(BF16)


def tables(shards, rows, per):
    total = shards * rows
    k1 = bit_reversed(shards)
    outer = 2 * np.pi / shards * (np.outer(k1, np.arange(shards)) % shards)
    turn = 2 * np.pi / total * np.outer(k1, np.arange(rows))
    turn = np.tile(np.repeat(turn, per // 2, axis=0), (1, 2))
    inner = 2 * np.pi / rows * (np.outer(np.arange(rows), np.arange(rows)) % rows)
    across = np.kron(np.concatenate([np.cos(outer), -np.sin(outer)]), np.eye(per // 2))
    pair = np.eye(2)
    return (
        *halves(across),
        np.cos(turn).astype(np.float32),
        np.sin(turn).astype(np.float32),
        *halves(np.kron(pair, np.cos(inner))),
        *halves(np.kron(pair, np.sin(inner))),
    )


def operator_kernel(
    sizes,
    x_in, w_in, taps, freq_hbm, grad_hbm,
    across_hi, across_lo, turn_cos, turn_sin, cos_hi, cos_lo, sin_hi, sin_lo,
    gated, w_grad,
    x_all, w_all, total, query, freq_in, freq_out, freq_all, grad_all,
    sig_out, sig_all, conv_out, conv_all, gated_all, part_out, part_all,
    local_sem, ring_send, ring_recv, twin_send, twin_recv, x_send, x_recv,
    halo_send, halo_recv, edge_send, edge_recv, freq_send, freq_recv,
    grad_send, grad_recv, grad_x_send, grad_x_recv, sig_send, sig_recv,
    conv_send, conv_recv, gated_send, gated_recv, part_send, part_recv,
):
    zs, ys, xs = sizes
    rows, depth = x_in.shape
    piece, flat = w_in.shape
    width = flat // 3
    half = width // 2
    shards = zs * ys * 2
    near = ys * 2
    first = 5 * flat // 12 // 128 * 128
    z, y, core, x = (lax.axis_index(a) for a in ("z", "y", "core", "ch"))
    turn = 1 - 2 * core
    wrap = lambda v, n: lax.rem(v + 2 * n, n)
    here = (z * ys + y) * 2 + core
    group = y * 2 + core

    def device(place):
        return {"z": place // near, "y": place // 2 % ys, "core": place % 2, "ch": x}

    def by_axis(axis, step):
        if axis == "z":
            return {"z": wrap(z + turn * step, zs), "y": y, "core": core, "ch": x}
        if axis == "y":
            return {"z": z, "y": wrap(y + turn * step, ys), "core": core, "ch": x}
        return {"z": z, "y": y, "core": core, "ch": lax.rem(x + step, xs)}

    def in_group(other):
        return {"z": z, "y": other // 2, "core": other % 2, "ch": x}

    twin = in_group(y * 2 + 1 - core)
    after, before = lax.rem(here + 1, shards), lax.rem(here + shards - 1, shards)
    peers = [by_axis("z", 1), by_axis("z", -1)]
    peers += [in_group(lax.rem(group + p, near)) for p in range(1, near)]
    peers += [by_axis("ch", d) for d in range(1, xs)] + [device(after), device(before)]
    barrier = pltpu.get_barrier_semaphore()
    for peer in peers:
        pl.semaphore_signal(barrier, inc=1, device_id=peer, device_id_type=MESH)
    pl.semaphore_wait(barrier, len(peers))

    def remote(src, dst, send, recv, to=twin):
        return pltpu.make_async_remote_copy(
            src_ref=src, dst_ref=dst, send_sem=send, recv_sem=recv,
            device_id=to, device_id_type=MESH,
        )

    sends = []

    def start(copy):
        copy.start()
        sends.append(copy)

    z_low, y_low = (zs - 1) // 2, (ys - 1) // 2
    columns = (slice(0, first), slice(first, flat))

    def place_of(fz, fy, of_core):
        zo, yo = wrap(z - turn * fz, zs), wrap(y - turn * fy, ys)
        return (zo * ys + yo) * 2 + of_core

    def slot(fz, fy, of_core):
        return pl.ds(pl.multiple_of(place_of(fz, fy, of_core) * piece, piece), piece)

    def ring_copy(part, origin, key, axis, step):
        where = slot(*origin, core)
        src = w_in.at[:, columns[part]] if origin == (0, 0) else w_all.at[where, columns[part]]
        sem = (part, key[0] + z_low, key[1] + y_low)
        return remote(
            src, w_all.at[where, columns[part]], ring_send.at[sem], ring_recv.at[sem],
            by_axis(axis, step),
        )

    def x_rows(of, n, row):
        return x_all.at[pl.ds(row, n), pl.ds(pl.multiple_of(of * depth, depth), depth)]

    def send_freq(place):
        remote(freq_out.at[place], freq_all.at[here], freq_send, freq_recv, device(place)).start()

    plan = ring_plan(zs, ys, first / flat)
    own_w = pltpu.make_async_copy(w_in, w_all.at[slot(0, 0, core)], local_sem.at[0])
    own_x = pltpu.make_async_copy(x_in, x_rows(x, rows, HALO), local_sem.at[1])
    load_freq = pltpu.make_async_copy(freq_hbm, freq_in, local_sem.at[2])

    share = rows // xs
    mine = pl.ds(pl.multiple_of(share * x, share), share)
    blocks = zs // 2

    def grad_piece(other, k):
        column = ((other % 2 * blocks + k) * ys + other // 2) * 128
        return grad_hbm.at[mine, pl.ds(pl.multiple_of(column, 128), 128)]

    own_grad = [
        pltpu.make_async_copy(
            grad_piece(group, k), grad_all.at[group, mine, pl.ds(128 * k, 128)], local_sem.at[3 + k]
        )
        for k in range(blocks)
    ]

    def open_x():
        own_w.start()
        own_x.start()
        load_freq.start()
        for d in range(1, xs):
            start(remote(x_in, x_rows(x, rows, HALO), x_send.at[d - 1], x_recv.at[d - 1], by_axis("ch", d)))
        for copy in own_grad:
            copy.start()
        for p in range(1, near):
            other = lax.rem(group + p, near)
            for k in range(blocks):
                remote(
                    grad_piece(other, k), grad_all.at[group, mine, pl.ds(128 * k, 128)],
                    grad_send, grad_recv, in_group(other),
                ).start()

    def pass_halo():
        own_x.wait()
        remote(x_in.at[pl.ds(0, HALO)], x_rows(x, HALO, 0), edge_send, edge_recv).wait_recv()
        for d in range(1, xs):
            start(remote(x_rows(x, HALO, 0), x_rows(x, HALO, 0), halo_send.at[d - 1], halo_recv.at[d - 1], by_axis("ch", d)))

    def turn_freq():
        load_freq.wait()
        for p in range(2):
            stacked = jnp.concatenate([freq_in[p, :, 0:half], freq_in[p, :, half:width]], axis=0)
            freq_out[:, p] = stacked.T.astype(BF16).reshape(shards, 4, 2 * rows)
        freq_all[here] = freq_out[here]

    grad_arrivals = lambda: grad_all.at[pl.ds(0, near - 1), pl.ds(0, share)]

    def close_x():
        own_w.wait()
        for d in range(1, xs):
            of = lax.rem(x + xs - d, xs)
            remote(x_in, x_rows(of, rows, HALO), x_send.at[d - 1], x_recv.at[d - 1]).wait_recv()
        for d in range(1, xs):
            of = lax.rem(x + xs - d, xs)
            remote(x_rows(of, HALO, 0), x_rows(of, HALO, 0), halo_send.at[d - 1], halo_recv.at[d - 1]).wait_recv()
        for copy in own_grad:
            copy.wait()
        remote(grad_arrivals(), grad_arrivals(), grad_send, grad_recv).wait_recv()
        for d in range(1, xs):
            start(remote(
                grad_all.at[:, mine], grad_all.at[:, mine],
                grad_x_send.at[d - 1], grad_x_recv.at[d - 1], by_axis("ch", d),
            ))

    def finish_grad():
        for d in range(1, xs):
            of = lax.rem(x + xs - d, xs)
            theirs = grad_all.at[:, pl.ds(pl.multiple_of(share * of, share), share)]
            remote(theirs, theirs, grad_x_send.at[d - 1], grad_x_recv.at[d - 1]).wait_recv()

    span = near * piece

    def mirror(f, n):
        return f if 2 * f == n else -f

    def multiply(fz, opening):
        for fy in range(-y_low, ys // 2 + 1):
            sem = (mirror(fz, zs) + z_low, mirror(fy, ys) + y_low)
            where = slot(fz, fy, 1 - core)
            remote(w_all.at[where], w_all.at[where], twin_send.at[sem], twin_recv.at[sem]).wait_recv()
            send_freq(place_of(fz, fy, 1 - core))
        base = pl.multiple_of(wrap(z - turn * fz, zs) * span, span)
        left = x_all[:, pl.ds(base, span)]

        @pl.loop(0, flat // TILE)
        def _(tile):
            cols = pl.ds(pl.multiple_of(tile * TILE, TILE), TILE)
            part = jnp.dot(left, w_all[pl.ds(base, span), cols], preferred_element_type=F32)
            if opening:
                total[:, cols] = part
            else:
                total[:, cols] += part

    start(remote(x_in.at[pl.ds(rows - HALO, HALO)], x_rows(x, HALO, 0), edge_send, edge_recv, device(after)))
    arrived, pending, multiplied = set(), [], []
    turned = False
    for index, (part, fz, fy, onward) in enumerate(plan):
        where = slot(fz, fy, core)
        if (fz, fy) != (0, 0):
            sem = (part, fz + z_low, fy + y_low)
            piece_at = w_all.at[where, columns[part]]
            remote(piece_at, piece_at, ring_send.at[sem], ring_recv.at[sem]).wait_recv()
        for axis, step, key in onward:
            start(ring_copy(part, (fz, fy), key, axis, step))
        arrived.add((part, fz, fy))
        if (1 - part, fz, fy) in arrived:
            sem = (fz + z_low, fy + y_low)
            src = w_in if (fz, fy) == (0, 0) else w_all.at[where]
            start(remote(src, w_all.at[where], twin_send.at[sem], twin_recv.at[sem], twin))
        if index == 1:
            open_x()
        if index == 5:
            pass_halo()
        if index == 11:
            turn_freq()
            turned = True
            for part_, fz_, fy_ in arrived_in_order(plan, index):
                send_freq(place_of(fz_, fy_, core))
        elif turned and (1 - part, fz, fy) in arrived:
            send_freq(place_of(fz, fy, core))
        pending += sorted(
            (k for k in range(-z_low, zs // 2 + 1) if k not in multiplied and k not in pending
             and all((p, g, f) in arrived for p in (0, 1) for g in (k, mirror(k, zs))
                     for f in range(-y_low, ys // 2 + 1))),
            key=abs,
        )
        if pending and index >= MATMUL_FROM and index % 3 == 0:
            if not multiplied:
                close_x()
            multiplied.append(pending.pop(0))
            multiply(multiplied[-1], len(multiplied) == 1)
    for fz in pending:
        multiply(fz, False)

    total[0:HALO] = jnp.where(here == 0, 0.0, total[0:HALO])

    def short(j, at):
        cols = slice(j * width + at, j * width + at + half)
        return sum(
            taps[i : i + 1, cols]
            * total[HALO - i : HALO - i + rows, cols].astype(BF16).astype(F32)
            for i in range(3)
        )

    signal = jnp.concatenate([short(1, at) * short(2, at) for at in (0, half)], axis=0)
    sig_out[...] = signal.T.astype(BF16).reshape(shards, 4, 2 * rows)

    def exchange(out, into, send, recv):
        @pl.loop(1, shards)
        def _(d):
            to = lax.rem(here + d, shards)
            remote(out.at[to], into.at[here], send, recv, device(to)).start()

        into[here] = out[here]

    others = pl.ds(0, shards - 1)

    def arrivals(into, send, recv):
        remote(into.at[others], into.at[others], send, recv).wait_recv()

    exchange(sig_out, sig_all, sig_send, sig_recv)
    for at in (0, half):
        query[:, at : at + half] = short(0, at)
    arrivals(freq_all, freq_send, freq_recv)
    arrivals(sig_all, sig_send, sig_recv)

    lines = 4 * shards
    mul = functools.partial(jnp.dot, preferred_element_type=F32)

    def split(value):
        high = value.astype(BF16)
        return high, (value - high.astype(F32)).astype(BF16)

    def within(real, imag):
        high, low = split(jnp.concatenate([real, imag], axis=0))
        cos = mul(high, cos_hi[...]) + mul(low, cos_hi[...]) + mul(high, cos_lo[...])
        sin = mul(high, sin_hi[...]) + mul(low, sin_hi[...]) + mul(high, sin_lo[...])
        return cos[:lines], cos[lines:], sin[:lines], sin[lines:]

    data = sig_all[...].reshape(lines, 2 * rows)
    data = mul(across_hi[...], data) + mul(across_lo[...], data)
    real, imag = data[:lines], data[lines:]
    real_cos, imag_cos, real_sin, imag_sin = within(
        real * turn_cos[...] + imag * turn_sin[...], imag * turn_cos[...] - real * turn_sin[...]
    )
    real, imag = real_cos + imag_sin, imag_cos - real_sin
    freq_real = freq_all[:, 0].reshape(lines, 2 * rows).astype(F32)
    freq_imag = freq_all[:, 1].reshape(lines, 2 * rows).astype(F32)
    real_cos, imag_cos, real_sin, imag_sin = within(
        real * freq_real - imag * freq_imag, real * freq_imag + imag * freq_real
    )
    real, imag = real_cos - imag_sin, imag_cos + real_sin
    high, low = split(jnp.concatenate(
        [real * turn_cos[...] - imag * turn_sin[...], imag * turn_cos[...] + real * turn_sin[...]],
        axis=0,
    ))
    back = lambda a, b: lax.dot_general(a, b, (((0,), (0,)), ((), ())), preferred_element_type=F32)
    data = back(across_hi[...], high) + back(across_hi[...], low) + back(across_lo[...], high)
    conv_out[...] = (data * (1 / (shards * rows))).astype(BF16).reshape(shards, 4, 2 * rows)
    exchange(conv_out, conv_all, conv_send, conv_recv)
    finish_grad()
    arrivals(conv_all, conv_send, conv_recv)

    conv = conv_all[...].reshape(lines, 2 * rows).astype(F32).T
    for n, at in enumerate((0, half)):
        value = (query[:, at : at + half] * conv[n * rows : (n + 1) * rows]).astype(BF16)
        gated_all[group, :, at : at + half] = value
    for p in range(1, near):
        start(remote(
            gated_all.at[group], gated_all.at[group], gated_send.at[p - 1], gated_recv.at[p - 1],
            in_group(lax.rem(group + p, near)),
        ))
    gated[...] = gated_all[group]
    for p in range(1, near):
        theirs = gated_all.at[lax.rem(group + near - p, near)]
        remote(theirs, theirs, gated_send.at[p - 1], gated_recv.at[p - 1]).wait_recv()
    right = gated_all[...].reshape(near * rows, width)
    count = part_out.shape[1]
    for k in range(blocks):
        left = grad_all[:, :, 128 * k : 128 * (k + 1)].reshape(near * rows, 128)
        part = back(left, right).astype(BF16)
        to_z = core * blocks + k
        for c in range(2):
            part_out[2 * k + c] = part[c * count : (c + 1) * count]
            stays = jnp.logical_and(to_z == z, core == c)

            @pl.when(stays)
            def _():
                part_all[z] = part_out[2 * k + c]

            @pl.when(jnp.logical_not(stays))
            def _():
                remote(
                    part_out.at[2 * k + c], part_all.at[z], part_send, part_recv,
                    {"z": to_z, "y": y, "core": c, "ch": x},
                ).start()
    keeps = core == z // blocks

    def close_parts(number):
        some = part_all.at[pl.ds(0, number)]
        copy = remote(some, some, part_send, part_recv)
        copy.wait_recv()
        copy.wait_send()

    @pl.when(keeps)
    def _():
        close_parts(zs - 1)

    @pl.when(jnp.logical_not(keeps))
    def _():
        close_parts(zs)

    w_grad[...] = sum(part_all[k].astype(F32) for k in range(zs))

    for copy in sends:
        copy.wait_send()
    remote(grad_arrivals(), grad_arrivals(), grad_send, grad_recv).wait_send()
    for into, send, recv in (
        (freq_all, freq_send, freq_recv), (sig_all, sig_send, sig_recv), (conv_all, conv_send, conv_recv)
    ):
        remote(into.at[others], into.at[others], send, recv).wait_send()


def arrived_in_order(plan, index):
    seen, done = set(), []
    for part, fz, fy, _ in plan[: index + 1]:
        if (1 - part, fz, fy) in seen and (fz, fy) != (0, 0):
            done.append((part, fz, fy))
        seen.add((part, fz, fy))
    return done


def on_device(features, w_in, short_filter, filter_spectrum, out_grad):
    zs, ys, xs = sizes = tuple(lax.axis_size(a) for a in ("z", "y", "ch"))
    rows, depth = features.shape
    piece, _, width = w_in.shape
    flat = 3 * width
    shards, near = zs * ys * 2, ys * 2
    per = width // shards
    message = (shards, per // 2, 2 * rows)
    count = out_grad.shape[1] // shards
    dma = pltpu.SemaphoreType.DMA
    vmem = pl.BlockSpec(memory_space=pltpu.VMEM)
    hbm = pl.BlockSpec(memory_space=pl.ANY)
    fixed = [jnp.asarray(t) for t in tables(shards, rows, per)]
    return pl.pallas_call(
        functools.partial(operator_kernel, sizes),
        out_shape=(
            jax.ShapeDtypeStruct((rows, width), BF16),
            jax.ShapeDtypeStruct((count, width), F32),
        ),
        in_specs=[vmem] * 3 + [hbm] * 2 + [vmem] * len(fixed),
        out_specs=(vmem, vmem),
        scratch_shapes=[
            pltpu.VMEM((rows + HALO, depth * xs), BF16),
            pltpu.VMEM((piece * shards, flat), BF16),
            pltpu.VMEM((rows + HALO, flat), F32),
            pltpu.VMEM((rows, width), F32),
            pltpu.VMEM((2, rows, width), F32),
            pltpu.VMEM((shards, 2, *message[1:]), BF16),
            pltpu.VMEM((shards, 2, *message[1:]), BF16),
            pltpu.VMEM((near, rows, zs // 2 * 128), BF16),
            *[pltpu.VMEM(message, BF16)] * 4,
            pltpu.VMEM((near, rows, width), BF16),
            pltpu.VMEM((zs, count, width), BF16),
            pltpu.VMEM((zs, count, width), BF16),
            dma((3 + zs // 2,)), dma((2, zs, ys)), dma((2, zs, ys)), dma((zs, ys)), dma((zs, ys)),
            dma((xs - 1,)), dma((xs - 1,)), dma((xs - 1,)), dma((xs - 1,)), dma, dma, dma, dma,
            dma, dma, dma((xs - 1,)), dma((xs - 1,)), dma, dma,
            dma, dma, dma((near - 1,)), dma((near - 1,)), dma, dma,
        ],
        compiler_params=pltpu.CompilerParams(
            collective_id=0, has_side_effects=True, vmem_limit_bytes=56 << 20
        ),
        name="operator",
    )(
        features, w_in.reshape(piece, flat), short_filter.reshape(3, flat),
        filter_spectrum, out_grad, *fixed,
    )


def solution(mesh):
    fine = Mesh(mesh.devices.reshape(8, 4, 2, 4), ("z", "y", "core", "ch"))
    in_specs = (
        P(CTX, "ch"),
        P(CTX, None, "ch"),
        P(None, None, "ch"),
        P(None, CTX, "ch"),
        P(CTX, None),
    )
    out_specs = (P(CTX, "ch"), P(CTX, "ch"))
    return jax.shard_map(
        on_device, mesh=fine, in_specs=in_specs, out_specs=out_specs, check_vma=False
    )
```

```python
import functools
import heapq

import jax
import jax.numpy as jnp
import numpy as np
from jax import lax
from jax.experimental import pallas as pl
from jax.experimental.pallas import tpu as pltpu
from jax.sharding import Mesh, PartitionSpec as P

CTX = ("z", "y", "core")
MESH = pl.DeviceIdType.MESH
HALO = 16
TILE = 256
MATMUL_FROM = 36
FREQ_FROM = 58
F32 = jnp.float32
BF16 = jnp.bfloat16


def ring_plan(zs, ys, share):
    z_max, z_min = zs // 2, -((zs - 1) // 2)
    y_max, y_min = ys // 2, -((ys - 1) // 2)
    size = {0: share * 2.1, 1: (1 - share) * 2.1}

    def steps(at, low, high):
        if at == 0:
            return [d for d, ok in ((1, high > 0), (-1, low < 0)) if ok]
        return [1] if 0 < at < high else [-1] if low < at < 0 else []

    def onward(part, fz, fy):
        along_z = [("z", d, (fz + d, fy)) for d in steps(fz, z_min, z_max)]
        along_y = [("y", d, (fz, fy + d)) for d in steps(fy, y_min, y_max)]
        if part == 0:
            return (along_y if fz == 0 else []) + along_z
        return (along_z if fy == 0 else []) + along_y

    free = {"y": 0.0, "z": 0.0}
    order, count = [], 2
    waiting = [(0.0, 0, 1, 0, 0), (0.0, 1, 0, 0, 0)]
    while waiting:
        now, _, part, fz, fy = heapq.heappop(waiting)
        sends = onward(part, fz, fy)
        order.append((part, fz, fy, sends))
        for axis, _, key in sends:
            free[axis] = max(free[axis], now) + size[part]
            count += 1
            heapq.heappush(waiting, (free[axis] + 1.7, count, part, *key))
    return order


def bit_reversed(count):
    bits = count.bit_length() - 1
    return np.array([int(format(i, f"0{bits}b")[::-1], 2) for i in range(count)])


def halves(table):
    high = table.astype(BF16)
    return high, (table - high.astype(np.float64)).astype(BF16)


def tables(shards, rows, per):
    total = shards * rows
    k1 = bit_reversed(shards)
    outer = 2 * np.pi / shards * (np.outer(k1, np.arange(shards)) % shards)
    turn = 2 * np.pi / total * np.outer(k1, np.arange(rows))
    turn = np.tile(np.repeat(turn, per, axis=0), (2, 1))
    inner = 2 * np.pi / rows * (np.outer(np.arange(rows), np.arange(rows)) % rows)
    across = np.kron(np.concatenate([np.cos(outer), -np.sin(outer)]), np.eye(per))
    return (
        np.stack(halves(across)),
        np.stack([np.cos(turn), np.sin(turn)]).astype(np.float32),
        np.stack([*halves(np.cos(inner)), *halves(np.sin(inner))]),
    )


def operator_kernel(
    sizes,
    x_in, w_in, taps, freq_hbm, grad_hbm, across_hbm, turn_hbm, inner_hbm,
    gated, w_grad,
    x_all, w_all, total, query, freq_in, freq_out, freq_all, freq_wide, grad_all, grad_turned,
    sig_out, sig_all, conv_out, conv_all, gated_all, part_out, part_all, across, turns, inner,
    local_sem, ring_send, ring_recv, twin_send, twin_recv, x_send, x_recv,
    halo_send, halo_recv, edge_send, edge_recv, freq_send, freq_recv,
    grad_send, grad_recv, grad_x_send, grad_x_recv, sig_send, sig_recv,
    conv_send, conv_recv, gated_send, gated_recv, part_send, part_recv,
):
    zs, ys, xs = sizes
    rows, depth = x_in.shape
    _, piece, width = w_in.shape
    flat = 3 * width
    half, quarter = width // 2, width // 4
    shards = zs * ys * 2
    near = ys * 2
    first = 5 * flat // 12 // 128 * 128
    z, y, core, x = (lax.axis_index(a) for a in ("z", "y", "core", "ch"))
    turn = 1 - 2 * core
    wrap = lambda v, n: lax.rem(v + 2 * n, n)
    here = (z * ys + y) * 2 + core
    group = y * 2 + core

    def device(place):
        return {"z": place // near, "y": place // 2 % ys, "core": place % 2, "ch": x}

    def by_axis(axis, step):
        if axis == "z":
            return {"z": wrap(z + turn * step, zs), "y": y, "core": core, "ch": x}
        if axis == "y":
            return {"z": z, "y": wrap(y + turn * step, ys), "core": core, "ch": x}
        return {"z": z, "y": y, "core": core, "ch": lax.rem(x + step, xs)}

    def in_group(other):
        return {"z": z, "y": other // 2, "core": other % 2, "ch": x}

    twin = in_group(y * 2 + 1 - core)
    after, before = lax.rem(here + 1, shards), lax.rem(here + shards - 1, shards)
    peers = [by_axis("z", 1), by_axis("z", -1), by_axis("y", 1), by_axis("y", -1), twin]
    peers += [by_axis("ch", d) for d in range(1, xs)] + [device(after), device(before)]
    barrier = pltpu.get_barrier_semaphore()
    for peer in peers:
        pl.semaphore_signal(barrier, inc=1, device_id=peer, device_id_type=MESH)

    z_low, y_low = (zs - 1) // 2, (ys - 1) // 2
    columns = (slice(0, first), slice(first, flat))

    def place_of(fz, fy, of_core):
        zo, yo = wrap(z - turn * fz, zs), wrap(y - turn * fy, ys)
        return (zo * ys + yo) * 2 + of_core

    def slot(fz, fy, of_core):
        return pl.ds(pl.multiple_of(place_of(fz, fy, of_core) * piece, piece), piece)

    def x_rows(of, n, row):
        return x_all.at[pl.ds(row, n), pl.ds(pl.multiple_of(of * depth, depth), depth)]

    share = rows // xs
    mine = pl.ds(pl.multiple_of(share * x, share), share)
    blocks = zs // 2

    def grad_piece(other, k):
        column = ((other % 2 * blocks + k) * ys + other // 2) * 128
        return grad_hbm.at[mine, pl.ds(pl.multiple_of(column, 128), 128)]

    def local(src, dst, n):
        copy = pltpu.make_async_copy(src, dst, local_sem.at[n])
        copy.start()
        return copy

    own_x = local(x_in, x_rows(x, rows, HALO), 0)
    load_freq = local(freq_hbm, freq_in, 1)
    loads = [
        local(src, dst, 2 + n)
        for n, (src, dst) in enumerate(((across_hbm, across), (turn_hbm, turns), (inner_hbm, inner)))
    ]
    loads += [
        local(grad_piece(group, k), grad_all.at[group, mine, pl.ds(128 * k, 128)], 5 + k)
        for k in range(blocks)
    ]
    for j in range(3):
        w_all[slot(0, 0, core), j * width : (j + 1) * width] = w_in[j]

    pl.semaphore_wait(barrier, len(peers))

    def remote(src, dst, send, recv, to=twin):
        return pltpu.make_async_remote_copy(
            src_ref=src, dst_ref=dst, send_sem=send, recv_sem=recv,
            device_id=to, device_id_type=MESH,
        )

    sends = []

    def start(copy):
        copy.start()
        sends.append(copy)

    def ring_copy(part, origin, key, axis, step):
        where = w_all.at[slot(*origin, core), columns[part]]
        sem = (part, key[0] + z_low, key[1] + y_low)
        return remote(where, where, ring_send.at[sem], ring_recv.at[sem], by_axis(axis, step))

    def open_x():
        start(remote(
            x_in.at[pl.ds(rows - HALO, HALO)], x_rows(x, HALO, 0), edge_send, edge_recv, device(after)
        ))
        for d in range(1, xs):
            start(remote(x_in, x_rows(x, rows, HALO), x_send.at[d - 1], x_recv.at[d - 1], by_axis("ch", d)))

    def pass_halo():
        own_x.wait()
        remote(x_in.at[pl.ds(0, HALO)], x_rows(x, HALO, 0), edge_send, edge_recv).wait_recv()
        for d in range(1, xs):
            own = x_rows(x, HALO, 0)
            start(remote(own, own, halo_send.at[d - 1], halo_recv.at[d - 1], by_axis("ch", d)))

    def close_x():
        for n, row, send, recv in ((rows, HALO, x_send, x_recv), (HALO, 0, halo_send, halo_recv)):
            for d in range(1, xs):
                theirs = x_rows(lax.rem(x + xs - d, xs), n, row)
                remote(theirs, theirs, send.at[d - 1], recv.at[d - 1]).wait_recv()

    def turn_freq():
        load_freq.wait()
        for h in range(2):
            for p in range(2):
                stacked = jnp.concatenate(
                    [freq_in[p, :, at : at + quarter] for at in (h * half, h * half + quarter)], axis=0
                )
                freq_out[:, h, p] = stacked.T.astype(BF16).reshape(shards, 2, 2 * rows)
        freq_all[here] = freq_out[here]

    later = []

    def send_freq(*key):
        later.append(key)
        if index >= FREQ_FROM:
            for each in later:
                place = place_of(*each)
                remote(freq_out.at[place], freq_all.at[here], freq_send, freq_recv, device(place)).start()
            later.clear()

    span = near * piece

    def mirror(f, n):
        return f if 2 * f == n else -f

    def meet(fz):
        for fy in range(-y_low, ys // 2 + 1):
            sem = (mirror(fz, zs) + z_low, mirror(fy, ys) + y_low)
            where = w_all.at[slot(fz, fy, 1 - core)]
            remote(where, where, twin_send.at[sem], twin_recv.at[sem]).wait_recv()
            send_freq(fz, fy, 1 - core)

    def multiply(fz, opening, tiles):
        base = pl.multiple_of(wrap(z - turn * fz, zs) * span, span)
        left = x_all[:, pl.ds(base, span)]
        begin, step, count = tiles

        @pl.loop(0, count)
        def _(n):
            cols = pl.ds(pl.multiple_of((begin + step * n) * TILE, TILE), TILE)
            part = jnp.dot(left, w_all[pl.ds(base, span), cols], preferred_element_type=F32)
            if opening:
                total[:, cols] = part
            else:
                total[:, cols] += part

    plan = ring_plan(zs, ys, first / flat)
    arrived, pending, multiplied = set(), [], []
    for index, (part, fz, fy, onward) in enumerate(plan):
        if (fz, fy) != (0, 0):
            sem = (part, fz + z_low, fy + y_low)
            where = w_all.at[slot(fz, fy, core), columns[part]]
            remote(where, where, ring_send.at[sem], ring_recv.at[sem]).wait_recv()
        for axis, step, key in onward:
            start(ring_copy(part, (fz, fy), key, axis, step))
        arrived.add((part, fz, fy))
        if (1 - part, fz, fy) in arrived:
            sem = (fz + z_low, fy + y_low)
            where = w_all.at[slot(fz, fy, core)]
            start(remote(where, where, twin_send.at[sem], twin_recv.at[sem], twin))
            if (fz, fy) != (0, 0):
                send_freq(fz, fy, core)
        if index == 1:
            open_x()
        if index == 5:
            pass_halo()
        if index == 11:
            turn_freq()
        pending += sorted(
            (k for k in range(-z_low, zs // 2 + 1) if k not in multiplied and k not in pending
             and all((p, g, f) in arrived for p in (0, 1) for g in (k, mirror(k, zs))
                     for f in range(-y_low, ys // 2 + 1))),
            key=abs,
        )
        if pending and index >= MATMUL_FROM and index % 3 == 0:
            if not multiplied:
                close_x()
            multiplied.append(pending.pop(0))
            meet(multiplied[-1])
            multiply(multiplied[-1], len(multiplied) == 1, (0, 1, flat // TILE))
    for fz in pending:
        meet(fz)

    def short(j, at):
        cols = slice(j * width + at, j * width + at + half)
        total[0:HALO, cols] = jnp.where(here == 0, 0.0, total[0:HALO, cols])
        return sum(
            taps[i, j : j + 1, at : at + half]
            * total[HALO - i : HALO - i + rows, cols].astype(BF16).astype(F32)
            for i in range(3)
        )

    def exchange(h, out, into, send, recv):
        @pl.loop(1, shards)
        def _(d):
            to = lax.rem(here + d, shards)
            remote(out.at[h, to], into.at[h, here], send.at[h], recv.at[h], device(to)).start()

        into[h, here] = out[h, here]

    others = pl.ds(0, shards - 1)

    def arrivals(h, into, send, recv):
        remote(into.at[h, others], into.at[h, others], send.at[h], recv.at[h]).wait_recv()

    for h in range(2):
        for fz in pending:
            multiply(fz, False, (2 + h, 2, 2))
        signal = short(1, h * half) * short(2, h * half)
        stacked = jnp.concatenate([signal[:, :quarter], signal[:, quarter:]], axis=0)
        sig_out[h] = stacked.T.astype(BF16).reshape(shards, 2, 2 * rows)
        exchange(h, sig_out, sig_all, sig_send, sig_recv)
    for p in range(1, near):
        other = lax.rem(group + p, near)
        for k in range(blocks):
            remote(
                grad_piece(other, k), grad_all.at[group, mine, pl.ds(128 * k, 128)],
                grad_send, grad_recv, in_group(other),
            ).start()
    for fz in pending:
        multiply(fz, False, (0, 1, 2))
    for at in (0, half):
        query[:, at : at + half] = short(0, at)
    for copy in loads:
        copy.wait()

    lines = 2 * shards
    blocks_of = (slice(0, rows), slice(rows, 2 * rows))
    mul = functools.partial(jnp.dot, preferred_element_type=F32)
    back = lambda a, b: lax.dot_general(a, b, (((0,), (0,)), ((), ())), preferred_element_type=F32)
    join = functools.partial(jnp.concatenate, axis=0)

    def split(value):
        high = value.astype(BF16)
        return high, (value - high.astype(F32)).astype(BF16)

    def within(real, imag):
        high, low = split(join([real, imag]))
        cos = mul(high, inner[0]) + mul(low, inner[0]) + mul(high, inner[1])
        sin = mul(high, inner[2]) + mul(low, inner[2]) + mul(high, inner[3])
        return cos[: 2 * lines], cos[2 * lines :], sin[: 2 * lines], sin[2 * lines :]

    def convolve(h):
        data = [sig_all[h, :, :, u].reshape(lines, rows) for u in blocks_of]
        data = [mul(across[0], d) + mul(across[1], d) for d in data]
        real, imag = join([d[:lines] for d in data]), join([d[lines:] for d in data])
        cos, sin = turns[0], turns[1]
        real_cos, imag_cos, real_sin, imag_sin = within(
            real * cos + imag * sin, imag * cos - real * sin
        )
        real, imag = real_cos + imag_sin, imag_cos - real_sin
        freq_real, freq_imag = freq_wide[h, 0], freq_wide[h, 1]
        real_cos, imag_cos, real_sin, imag_sin = within(
            real * freq_real - imag * freq_imag, real * freq_imag + imag * freq_real
        )
        real, imag = real_cos - imag_sin, imag_cos + real_sin
        real, imag = real * cos - imag * sin, imag * cos + real * sin
        for n, u in enumerate(blocks_of):
            own = slice(n * lines, (n + 1) * lines)
            high, low = split(join([real[own], imag[own]]))
            data = back(across[0], high) + back(across[0], low) + back(across[1], high)
            data = (data * (1 / (shards * rows))).astype(BF16)
            conv_out[h, :, :, u] = data.reshape(shards, 2, rows)
        exchange(h, conv_out, conv_all, conv_send, conv_recv)

    remote(freq_all.at[others], freq_all.at[others], freq_send, freq_recv).wait_recv()
    for h in range(2):
        for p in range(2):
            freq_wide[h, p] = join(
                [freq_all[:, h, p, :, u].reshape(lines, rows).astype(F32) for u in blocks_of]
            )
    for h in range(2):
        arrivals(h, sig_all, sig_send, sig_recv)
        convolve(h)

    grad_arrivals = grad_all.at[pl.ds(0, near - 1), pl.ds(0, share)]
    remote(grad_arrivals, grad_arrivals, grad_send, grad_recv).wait_recv()
    for d in range(1, xs):
        own = grad_all.at[:, mine]
        start(remote(own, own, grad_x_send.at[d - 1], grad_x_recv.at[d - 1], by_axis("ch", d)))

    def gate(h):
        arrivals(h, conv_all, conv_send, conv_recv)
        conv = conv_all[h].reshape(lines, 2 * rows).astype(F32).T
        for n in range(2):
            at = h * half + n * quarter
            value = query[:, at : at + quarter] * conv[n * rows : (n + 1) * rows]
            gated_all[h, group, :, n * quarter : (n + 1) * quarter] = value.astype(BF16)
        for p in range(1, near):
            own = gated_all.at[h, group]
            start(remote(
                own, own, gated_send.at[h, p - 1], gated_recv.at[h, p - 1],
                in_group(lax.rem(group + p, near)),
            ))
        gated[:, h * half : (h + 1) * half] = gated_all[h, group]

    for h in range(2):
        gate(h)
    for d in range(1, xs):
        of = lax.rem(x + xs - d, xs)
        theirs = grad_all.at[:, pl.ds(pl.multiple_of(share * of, share), share)]
        remote(theirs, theirs, grad_x_send.at[d - 1], grad_x_recv.at[d - 1]).wait_recv()
    grad_turned[...] = grad_all[...].reshape(near * rows, blocks * 128).T
    count = part_out.shape[2]
    for h in range(2):
        for p in range(1, near):
            theirs = gated_all.at[h, lax.rem(group + near - p, near)]
            remote(theirs, theirs, gated_send.at[h, p - 1], gated_recv.at[h, p - 1]).wait_recv()
        right = gated_all[h].reshape(near * rows, half)
        for k in range(blocks):
            part = mul(grad_turned[128 * k : 128 * (k + 1)], right).astype(BF16)
            to_z = core * blocks + k
            for c in range(2):
                part_out[h, 2 * k + c] = part[c * count : (c + 1) * count]
                stays = jnp.logical_and(to_z == z, core == c)

                @pl.when(stays)
                def _():
                    part_all[h, z] = part_out[h, 2 * k + c]

                @pl.when(jnp.logical_not(stays))
                def _():
                    remote(
                        part_out.at[h, 2 * k + c], part_all.at[h, z], part_send.at[h], part_recv.at[h],
                        {"z": to_z, "y": y, "core": c, "ch": x},
                    ).start()
    keeps = core == z // blocks

    def close_parts(h, number):
        some = part_all.at[h, pl.ds(0, number)]
        copy = remote(some, some, part_send.at[h], part_recv.at[h])
        copy.wait_recv()
        copy.wait_send()

    for h in range(2):

        @pl.when(keeps)
        def _():
            close_parts(h, zs - 1)

        @pl.when(jnp.logical_not(keeps))
        def _():
            close_parts(h, zs)

        w_grad[:, h * half : (h + 1) * half] = sum(part_all[h, k].astype(F32) for k in range(zs))

    for copy in sends:
        copy.wait_send()
    remote(grad_arrivals, grad_arrivals, grad_send, grad_recv).wait_send()
    remote(freq_all.at[others], freq_all.at[others], freq_send, freq_recv).wait_send()
    for h in range(2):
        for into, send, recv in ((sig_all, sig_send, sig_recv), (conv_all, conv_send, conv_recv)):
            remote(into.at[h, others], into.at[h, others], send.at[h], recv.at[h]).wait_send()


def settle_kernel(a, b, a_out, b_out):
    a_out[...] = a[...]
    b_out[...] = b[...]


def on_device(features, w_in, short_filter, filter_spectrum, out_grad):
    zs, ys, xs = sizes = tuple(lax.axis_size(a) for a in ("z", "y", "ch"))
    rows, depth = features.shape
    piece, _, width = w_in.shape
    flat = 3 * width
    half = width // 2
    shards, near = zs * ys * 2, ys * 2
    per = half // shards // 2
    message = (2, shards, per, 2 * rows)
    count = out_grad.shape[1] // shards
    dma = pltpu.SemaphoreType.DMA
    vmem = pl.BlockSpec(memory_space=pltpu.VMEM)
    hbm = pl.BlockSpec(memory_space=pl.ANY)
    fixed = [jnp.asarray(t) for t in tables(shards, rows, per)]
    outs = (
        jax.ShapeDtypeStruct((rows, width), BF16),
        jax.ShapeDtypeStruct((count, width), F32),
    )
    results = pl.pallas_call(
        functools.partial(operator_kernel, sizes),
        out_shape=outs,
        in_specs=[vmem] * 3 + [hbm] * 5,
        out_specs=(vmem, vmem),
        scratch_shapes=[
            pltpu.VMEM((rows + HALO, depth * xs), BF16),
            pltpu.VMEM((piece * shards, flat), BF16),
            pltpu.VMEM((rows + HALO, flat), F32),
            pltpu.VMEM((rows, width), F32),
            pltpu.VMEM((2, rows, width), F32),
            pltpu.VMEM((shards, 2, 2, per, 2 * rows), BF16),
            pltpu.VMEM((shards, 2, 2, per, 2 * rows), BF16),
            pltpu.VMEM((2, 2, 2 * per * shards, rows), F32),
            pltpu.VMEM((near, rows, zs // 2 * 128), BF16),
            pltpu.VMEM((zs // 2 * 128, near * rows), BF16),
            *[pltpu.VMEM(message, BF16)] * 4,
            pltpu.VMEM((2, near, rows, half), BF16),
            pltpu.VMEM((2, zs, count, half), BF16),
            pltpu.VMEM((2, zs, count, half), BF16),
            *[pltpu.VMEM(t.shape, t.dtype) for t in fixed],
            dma((5 + zs // 2,)), dma((2, zs, ys)), dma((2, zs, ys)), dma((zs, ys)), dma((zs, ys)),
            dma((xs - 1,)), dma((xs - 1,)), dma((xs - 1,)), dma((xs - 1,)), dma, dma, dma, dma,
            dma, dma, dma((xs - 1,)), dma((xs - 1,)), dma((2,)), dma((2,)),
            dma((2,)), dma((2,)), dma((2, near - 1)), dma((2, near - 1)), dma((2,)), dma((2,)),
        ],
        compiler_params=pltpu.CompilerParams(
            collective_id=0, has_side_effects=True, vmem_limit_bytes=56 << 20
        ),
        name="operator",
    )(features, w_in.transpose(1, 0, 2), short_filter, filter_spectrum, out_grad, *fixed)
    return pl.pallas_call(
        settle_kernel, out_shape=outs, in_specs=[vmem] * 2, out_specs=(vmem, vmem), name="settle"
    )(*results)


def solution(mesh):
    fine = Mesh(mesh.devices.reshape(8, 4, 2, 4), ("z", "y", "core", "ch"))
    in_specs = (
        P(CTX, "ch"),
        P(CTX, None, "ch"),
        P(None, None, "ch"),
        P(None, CTX, "ch"),
        P(CTX, None),
    )
    out_specs = (P(CTX, "ch"), P(CTX, "ch"))
    return jax.shard_map(
        on_device, mesh=fine, in_specs=in_specs, out_specs=out_specs, check_vma=False
    )
```

```python
import functools
import heapq

import jax
import jax.numpy as jnp
import numpy as np
from jax import lax
from jax.experimental import pallas as pl
from jax.experimental.pallas import tpu as pltpu
from jax.sharding import Mesh, PartitionSpec as P

CTX = ("z", "y", "core")
MESH = pl.DeviceIdType.MESH
HALO = 16
TILE = 256
MATMUL_FROM = 36
FREQ_FROM = 11
GRAD_AT = 1
F32 = jnp.float32
BF16 = jnp.bfloat16


def ring_plan(zs, ys, share):
    z_max, z_min = zs // 2, -((zs - 1) // 2)
    y_max, y_min = ys // 2, -((ys - 1) // 2)
    size = {0: share * 2.1, 1: (1 - share) * 2.1}

    def steps(at, low, high):
        if at == 0:
            return [d for d, ok in ((1, high > 0), (-1, low < 0)) if ok]
        return [1] if 0 < at < high else [-1] if low < at < 0 else []

    def onward(part, fz, fy):
        along_z = [("z", d, (fz + d, fy)) for d in steps(fz, z_min, z_max)]
        along_y = [("y", d, (fz, fy + d)) for d in steps(fy, y_min, y_max)]
        if part == 0:
            return (along_y if fz == 0 else []) + along_z
        return (along_z if fy == 0 else []) + along_y

    free = {"y": 0.0, "z": 0.0}
    order, count = [], 2
    waiting = [(0.0, 0, 1, 0, 0), (0.0, 1, 0, 0, 0)]
    while waiting:
        now, _, part, fz, fy = heapq.heappop(waiting)
        sends = onward(part, fz, fy)
        order.append((part, fz, fy, sends))
        for axis, _, key in sends:
            free[axis] = max(free[axis], now) + size[part]
            count += 1
            heapq.heappush(waiting, (free[axis] + 1.7, count, part, *key))
    return order


def bit_reversed(count):
    bits = count.bit_length() - 1
    return np.array([int(format(i, f"0{bits}b")[::-1], 2) for i in range(count)])


def halves(table):
    high = table.astype(BF16)
    return high, (table - high.astype(np.float64)).astype(BF16)


def tables(shards, rows, per):
    total = shards * rows
    k1 = bit_reversed(shards)
    outer = 2 * np.pi / shards * (np.outer(k1, np.arange(shards)) % shards)
    turn = 2 * np.pi / total * np.outer(k1, np.arange(rows))
    turn = np.tile(np.repeat(turn, per, axis=0), (2, 1))
    inner = 2 * np.pi / rows * (np.outer(np.arange(rows), np.arange(rows)) % rows)
    across = np.kron(np.concatenate([np.cos(outer), -np.sin(outer)]), np.eye(per))
    return (
        np.stack(halves(across)),
        np.stack([np.cos(turn), np.sin(turn)]).astype(np.float32),
        np.stack([*halves(np.cos(inner)), *halves(np.sin(inner))]),
    )


def operator_kernel(
    sizes,
    x_in, w_in, taps_hbm, freq_hbm, grad_hbm, across_hbm, turn_hbm, inner_hbm,
    gated, w_grad,
    x_all, w_all, total, query, freq_in, freq_out, freq_all, freq_wide, grad_all, grad_turned,
    sig_out, sig_all, conv_out, conv_all, gated_all, part_out, part_all, relayed, across, turns, inner, taps,
    local_sem, ring_send, ring_recv, twin_send, twin_recv, x_send, x_recv,
    halo_send, halo_recv, edge_send, edge_recv, freq_send, freq_recv,
    grad_send, grad_recv, grad_x_send, grad_x_recv, sig_send, sig_recv,
    conv_send, conv_recv, gated_send, gated_recv, pair_send, pair_recv, part_send, part_recv, relay_send, relay_recv,
):
    zs, ys, xs = sizes
    rows, depth = x_in.shape
    _, piece, width = w_in.shape
    flat = 3 * width
    half, quarter = width // 2, width // 4
    shards = zs * ys * 2
    near = ys * 2
    first = 5 * flat // 12 // 128 * 128
    z, y, core, x = (lax.axis_index(a) for a in ("z", "y", "core", "ch"))
    turn = 1 - 2 * core
    wrap = lambda v, n: lax.rem(v + 2 * n, n)
    here = (z * ys + y) * 2 + core
    group = y * 2 + core

    def device(place):
        return {"z": place // near, "y": place // 2 % ys, "core": place % 2, "ch": x}

    def by_axis(axis, step):
        if axis == "z":
            return {"z": wrap(z + turn * step, zs), "y": y, "core": core, "ch": x}
        if axis == "y":
            return {"z": z, "y": wrap(y + turn * step, ys), "core": core, "ch": x}
        return {"z": z, "y": y, "core": core, "ch": lax.rem(x + step, xs)}

    def in_group(other):
        return {"z": z, "y": other // 2, "core": other % 2, "ch": x}

    twin = in_group(y * 2 + 1 - core)
    after, before = lax.rem(here + 1, shards), lax.rem(here + shards - 1, shards)
    peers = [by_axis("z", 1), by_axis("z", -1)]
    peers += [in_group(lax.rem(group + p, near)) for p in range(1, near)]
    peers += [by_axis("ch", d) for d in range(1, xs)] + [device(after), device(before)]
    barrier = pltpu.get_barrier_semaphore()
    for peer in peers:
        pl.semaphore_signal(barrier, inc=1, device_id=peer, device_id_type=MESH)

    z_low, y_low = (zs - 1) // 2, (ys - 1) // 2
    columns = (slice(0, first), slice(first, flat))

    def place_of(fz, fy, of_core):
        zo, yo = wrap(z - turn * fz, zs), wrap(y - turn * fy, ys)
        return (zo * ys + yo) * 2 + of_core

    def slot(fz, fy, of_core):
        return pl.ds(pl.multiple_of(place_of(fz, fy, of_core) * piece, piece), piece)

    def x_rows(of, n, row):
        return x_all.at[pl.ds(row, n), pl.ds(pl.multiple_of(of * depth, depth), depth)]

    share = rows // xs
    mine = pl.ds(pl.multiple_of(share * x, share), share)
    blocks = zs // 2

    def grad_piece(other, k):
        column = ((other % 2 * blocks + k) * ys + other // 2) * 128
        return grad_hbm.at[mine, pl.ds(pl.multiple_of(column, 128), 128)]

    def local(src, dst, n):
        copy = pltpu.make_async_copy(src, dst, local_sem.at[n])
        copy.start()
        return copy

    own_w = [
        local(w_in.at[j], w_all.at[slot(0, 0, core), pl.ds(j * width, width)], 6 + j) for j in range(3)
    ]
    own_x = local(x_in, x_rows(x, rows, HALO), 0)
    load_freq = local(freq_hbm, freq_in, 1)
    loads = [
        local(src, dst, 2 + n)
        for n, (src, dst) in enumerate(((across_hbm, across), (turn_hbm, turns), (inner_hbm, inner), (taps_hbm, taps)))
    ]
    loads += [
        local(grad_piece(group, k), grad_all.at[group, mine, pl.ds(128 * k, 128)], 9 + k)
        for k in range(blocks)
    ]
    for copy in own_w:
        copy.wait()
    pl.semaphore_wait(barrier, len(peers))

    def remote(src, dst, send, recv, to=twin):
        return pltpu.make_async_remote_copy(
            src_ref=src, dst_ref=dst, send_sem=send, recv_sem=recv,
            device_id=to, device_id_type=MESH,
        )

    sends = []

    def start(copy):
        copy.start()
        sends.append(copy)

    def ring_copy(part, origin, key, axis, step):
        where = w_all.at[slot(*origin, core), columns[part]]
        sem = (part, key[0] + z_low, key[1] + y_low)
        return remote(where, where, ring_send.at[sem], ring_recv.at[sem], by_axis(axis, step))

    def open_x():
        own_x.wait()
        start(remote(
            x_rows(x, HALO, rows), x_rows(x, HALO, 0), edge_send, edge_recv, device(after)
        ))
        for d in range(1, xs):
            start(remote(x_rows(x, rows, HALO), x_rows(x, rows, HALO), x_send.at[d - 1], x_recv.at[d - 1], by_axis("ch", d)))

    def send_grad():
        for p in range(1, near):
            other = lax.rem(group + p, near)
            for k in range(blocks):
                remote(
                    grad_piece(other, k), grad_all.at[group, mine, pl.ds(128 * k, 128)],
                    grad_send, grad_recv, in_group(other),
                ).start()

    grad_arrivals = grad_all.at[pl.ds(0, near - 1), pl.ds(0, share)]

    def pass_grad():
        for copy in loads:
            copy.wait()
        remote(grad_arrivals, grad_arrivals, grad_send, grad_recv).wait_recv()
        for d in range(1, xs):
            own = grad_all.at[:, mine]
            start(remote(own, own, grad_x_send.at[d - 1], grad_x_recv.at[d - 1], by_axis("ch", d)))

    def pass_halo():
        remote(x_rows(x, HALO, 0), x_rows(x, HALO, 0), edge_send, edge_recv).wait_recv()
        for d in range(1, xs):
            own = x_rows(x, HALO, 0)
            start(remote(own, own, halo_send.at[d - 1], halo_recv.at[d - 1], by_axis("ch", d)))

    def close_x():
        for n, row, send, recv in ((rows, HALO, x_send, x_recv), (HALO, 0, halo_send, halo_recv)):
            for d in range(1, xs):
                theirs = x_rows(lax.rem(x + xs - d, xs), n, row)
                remote(theirs, theirs, send.at[d - 1], recv.at[d - 1]).wait_recv()

    def turn_freq():
        load_freq.wait()
        for h in range(2):
            for p in range(2):
                stacked = jnp.concatenate(
                    [freq_in[p, :, at : at + quarter] for at in (h * half, h * half + quarter)], axis=0
                )
                freq_out[:, h, p] = stacked.T.astype(BF16).reshape(shards, 2, 2 * rows)
        freq_all[here] = freq_out[here]

    later = []

    def send_freq(*key):
        later.append(key)
        if index >= FREQ_FROM:
            for each in later:
                place = place_of(*each)
                remote(freq_out.at[place], freq_all.at[here], freq_send, freq_recv, device(place)).start()
            later.clear()

    span = near * piece

    def mirror(f, n):
        return f if 2 * f == n else -f

    def meet(fz):
        for fy in range(-y_low, ys // 2 + 1):
            sem = (mirror(fz, zs) + z_low, mirror(fy, ys) + y_low)
            where = w_all.at[slot(fz, fy, 1 - core)]
            remote(where, where, twin_send.at[sem], twin_recv.at[sem]).wait_recv()
            send_freq(fz, fy, 1 - core)

    def multiply(fz, opening, tiles):
        base = pl.multiple_of(wrap(z - turn * fz, zs) * span, span)
        left = x_all[:, pl.ds(base, span)]
        begin, step, count = tiles

        @pl.loop(0, count)
        def _(n):
            cols = pl.ds(pl.multiple_of((begin + step * n) * TILE, TILE), TILE)
            part = jnp.dot(left, w_all[pl.ds(base, span), cols], preferred_element_type=F32)
            if opening:
                total[:, cols] = part
            else:
                total[:, cols] += part

    plan = ring_plan(zs, ys, first / flat)
    arrived, pending, multiplied = set(), [], []
    for index, (part, fz, fy, onward) in enumerate(plan):
        if (fz, fy) != (0, 0):
            sem = (part, fz + z_low, fy + y_low)
            where = w_all.at[slot(fz, fy, core), columns[part]]
            remote(where, where, ring_send.at[sem], ring_recv.at[sem]).wait_recv()
        for axis, step, key in onward:
            start(ring_copy(part, (fz, fy), key, axis, step))
        arrived.add((part, fz, fy))
        if (1 - part, fz, fy) in arrived:
            sem = (fz + z_low, fy + y_low)
            where = w_all.at[slot(fz, fy, core)]
            start(remote(where, where, twin_send.at[sem], twin_recv.at[sem], twin))
            if (fz, fy) != (0, 0):
                send_freq(fz, fy, core)
        if index == 1:
            open_x()
        if index == GRAD_AT:
            send_grad()
        if index == 5:
            pass_halo()
        if index == 11:
            turn_freq()
        pending += sorted(
            (k for k in range(-z_low, zs // 2 + 1) if k not in multiplied and k not in pending
             and all((p, g, f) in arrived for p in (0, 1) for g in (k, mirror(k, zs))
                     for f in range(-y_low, ys // 2 + 1))),
            key=abs,
        )
        if pending and index >= MATMUL_FROM and index % 3 == 0:
            if not multiplied:
                close_x()
                pass_grad()
            multiplied.append(pending.pop(0))
            meet(multiplied[-1])
            multiply(multiplied[-1], len(multiplied) == 1, (0, 1, flat // TILE))
    for fz in pending:
        meet(fz)

    def short(j, at):
        cols = slice(j * width + at, j * width + at + half)
        total[0:HALO, cols] = jnp.where(here == 0, 0.0, total[0:HALO, cols])
        return sum(
            taps[i, j : j + 1, at : at + half]
            * total[HALO - i : HALO - i + rows, cols].astype(BF16).astype(F32)
            for i in range(3)
        )

    def exchange(h, out, into, send, recv):
        @pl.loop(1, shards)
        def _(d):
            to = lax.rem(here + d, shards)
            remote(out.at[h, to], into.at[h, here], send.at[h], recv.at[h], device(to)).start()

        into[h, here] = out[h, here]

    others = pl.ds(0, shards - 1)

    def arrivals(h, into, send, recv):
        remote(into.at[h, others], into.at[h, others], send.at[h], recv.at[h]).wait_recv()

    for h in range(2):
        for fz in pending:
            multiply(fz, False, (2 + h, 2, 2))
        signal = short(1, h * half) * short(2, h * half)
        stacked = jnp.concatenate([signal[:, :quarter], signal[:, quarter:]], axis=0)
        sig_out[h] = stacked.T.astype(BF16).reshape(shards, 2, 2 * rows)
        exchange(h, sig_out, sig_all, sig_send, sig_recv)
    for fz in pending:
        multiply(fz, False, (0, 1, 2))
    for at in (0, half):
        query[:, at : at + half] = short(0, at)

    lines = 2 * shards
    blocks_of = (slice(0, rows), slice(rows, 2 * rows))
    mul = functools.partial(jnp.dot, preferred_element_type=F32)
    back = lambda a, b: lax.dot_general(a, b, (((0,), (0,)), ((), ())), preferred_element_type=F32)
    join = functools.partial(jnp.concatenate, axis=0)

    def split(value):
        high = value.astype(BF16)
        return high, (value - high.astype(F32)).astype(BF16)

    def within(real, imag):
        high, low = split(join([real, imag]))
        cos = mul(high, inner[0]) + mul(low, inner[0]) + mul(high, inner[1])
        sin = mul(high, inner[2]) + mul(low, inner[2]) + mul(high, inner[3])
        return cos[: 2 * lines], cos[2 * lines :], sin[: 2 * lines], sin[2 * lines :]

    def convolve(h):
        data = [sig_all[h, :, :, u].reshape(lines, rows) for u in blocks_of]
        data = [mul(across[0], d) + mul(across[1], d) for d in data]
        real, imag = join([d[:lines] for d in data]), join([d[lines:] for d in data])
        cos, sin = turns[0], turns[1]
        real_cos, imag_cos, real_sin, imag_sin = within(
            real * cos + imag * sin, imag * cos - real * sin
        )
        real, imag = real_cos + imag_sin, imag_cos - real_sin
        freq_real, freq_imag = freq_wide[h, 0], freq_wide[h, 1]
        real_cos, imag_cos, real_sin, imag_sin = within(
            real * freq_real - imag * freq_imag, real * freq_imag + imag * freq_real
        )
        real, imag = real_cos - imag_sin, imag_cos + real_sin
        real, imag = real * cos - imag * sin, imag * cos + real * sin
        for n, u in enumerate(blocks_of):
            own = slice(n * lines, (n + 1) * lines)
            high, low = split(join([real[own], imag[own]]))
            data = back(across[0], high) + back(across[0], low) + back(across[1], high)
            data = (data * (1 / (shards * rows))).astype(BF16)
            conv_out[h, :, :, u] = data.reshape(shards, 2, rows)
        exchange(h, conv_out, conv_all, conv_send, conv_recv)

    remote(freq_all.at[others], freq_all.at[others], freq_send, freq_recv).wait_recv()
    for h in range(2):
        for p in range(2):
            freq_wide[h, p] = join(
                [freq_all[:, h, p, :, u].reshape(lines, rows).astype(F32) for u in blocks_of]
            )
    for h in range(2):
        arrivals(h, sig_all, sig_send, sig_recv)
        convolve(h)

    def gated_from(h, fy, of_core):
        return gated_all.at[h, wrap(y - turn * fy, ys) * 2 + of_core]

    def pass_gated(h, fy, step):
        block = gated_from(h, fy, core)
        sem = (h, y_low + (ys // 2 if 2 * abs(fy + step) == ys else fy + step))
        start(remote(block, block, gated_send.at[sem], gated_recv.at[sem], by_axis("y", step)))

    def pair_gated(h, fy):
        block, sem = gated_from(h, fy, core), (h, y_low + fy)
        start(remote(block, block, pair_send.at[sem], pair_recv.at[sem], twin))

    def take_gated(h, fy):
        block, sem = gated_from(h, fy, core), (h, y_low + fy)
        remote(block, block, gated_send.at[sem], gated_recv.at[sem]).wait_recv()
        if abs(fy) == 1 and fy == 1 - 2 * h:
            pass_gated(h, fy, fy)
        pair_gated(h, fy)

    def gate(h):
        arrivals(h, conv_all, conv_send, conv_recv)
        conv = conv_all[h].reshape(lines, 2 * rows).astype(F32).T
        for n in range(2):
            at = h * half + n * quarter
            value = query[:, at : at + quarter] * conv[n * rows : (n + 1) * rows]
            gated_all[h, group, :, n * quarter : (n + 1) * quarter] = value.astype(BF16)
        pass_gated(h, 0, 1)
        pass_gated(h, 0, -1)
        pair_gated(h, 0)
        gated[:, h * half : (h + 1) * half] = gated_all[h, group]

    for d in range(1, xs):
        of = lax.rem(x + xs - d, xs)
        theirs = grad_all.at[:, pl.ds(pl.multiple_of(share * of, share), share)]
        remote(theirs, theirs, grad_x_send.at[d - 1], grad_x_recv.at[d - 1]).wait_recv()
    grad_turned[...] = grad_all[...].reshape(near * rows, blocks * 128).T
    count = w_grad.shape[0]

    def distance(h, k):
        return lax.rem((1 - 2 * h) * (z - core * blocks - k) + 2 * zs, zs)

    def relay_copy(h, k, to, n):
        step = z - (1 - 2 * h) * to
        return remote(
            part_out.at[h, k], relayed.at[h, n], relay_send.at[h, k], relay_recv.at[h, n],
            {"z": wrap(step, zs), "y": y, "core": core, "ch": x},
        )

    def final_copy(h, k, c, n):
        return remote(
            part_out.at[h, k, pl.ds(c * count, count)], part_all.at[h, n],
            part_send.at[h, k, c], part_recv.at[h],
            {"z": core * blocks + k, "y": y, "core": c, "ch": x},
        )

    ends = {0: 0, 1: 1, zs - 1: 2, 2: 3, zs - 2: 4}
    relays = {3: (1, 0), 4: (2, 1), zs - 3: (-1, 2)}

    def send_part(h, k, away, act):
        for c in range(2):
            if away:
                act(final_copy(h, k, c, ends[away]))
            else:

                @pl.when(core != c)
                def _():
                    act(final_copy(h, k, c, 0))

    def products(h):
        for fy in range(-y_low, ys // 2 + 1):
            block, sem = gated_from(h, fy, 1 - core), (h, y_low + mirror(fy, ys))
            remote(block, block, pair_send.at[sem], pair_recv.at[sem]).wait_recv()
        right = gated_all[h].reshape(near * rows, half)
        for k in range(blocks):
            part_out[h, k] = mul(grad_turned[128 * k : 128 * (k + 1)], right).astype(BF16)
        for k in range(blocks):
            for away, (to, n) in relays.items():

                @pl.when(distance(h, k) == away)
                def _():
                    relay_copy(h, k, to, n).start()

        for k in range(blocks):
            for away in (1, zs - 1, 0):

                @pl.when(distance(h, k) == away)
                def _():
                    send_part(h, k, away, lambda copy: copy.start())
                    if not away:
                        part_all[h, 0] = part_out[h, k, pl.ds(pl.multiple_of(core * count, count), count)]

    def combine(h):
        for k in range(blocks):
            for away, inputs in ((2, (0, 1)), (zs - 2, (2,))):

                @pl.when(distance(h, k) == away)
                def _():
                    for n in inputs:
                        remote(
                            relayed.at[h, n], relayed.at[h, n], relay_send.at[h, k], relay_recv.at[h, n]
                        ).wait_recv()
                    total_part = part_out[h, k].astype(F32)
                    for n in inputs:
                        total_part += relayed[h, n].astype(F32)
                    part_out[h, k] = total_part.astype(BF16)
                    send_part(h, k, away, lambda copy: copy.start())

    gate(0)
    take_gated(0, 1)
    take_gated(0, -1)
    gate(1)
    take_gated(0, 2)
    products(0)
    take_gated(1, -1)
    take_gated(1, 1)
    combine(0)
    take_gated(1, 2)
    products(1)
    combine(1)
    keeps = core == z // blocks

    def close_parts(h, number):
        some = part_all.at[h, pl.ds(0, number)]
        remote(some, some, part_send.at[h, 0, 0], part_recv.at[h]).wait_recv()

    for h in range(2):

        @pl.when(keeps)
        def _():
            close_parts(h, len(ends) - 1)

        @pl.when(jnp.logical_not(keeps))
        def _():
            close_parts(h, len(ends))

        w_grad[:, h * half : (h + 1) * half] = sum(part_all[h, n].astype(F32) for n in range(len(ends)))
        for k in range(blocks):
            for away in range(zs):

                @pl.when(distance(h, k) == away)
                def _():
                    if away in relays:
                        relay_copy(h, k, *relays[away]).wait_send()
                    else:
                        send_part(h, k, away, lambda copy: copy.wait_send())

    for copy in sends:
        copy.wait_send()
    remote(grad_arrivals, grad_arrivals, grad_send, grad_recv).wait_send()
    remote(freq_all.at[others], freq_all.at[others], freq_send, freq_recv).wait_send()
    for h in range(2):
        for into, send, recv in ((sig_all, sig_send, sig_recv), (conv_all, conv_send, conv_recv)):
            remote(into.at[h, others], into.at[h, others], send.at[h], recv.at[h]).wait_send()


def settle_kernel(a, b, a_out, b_out):
    a_out[...] = a[...]
    b_out[...] = b[...]


def on_device(features, w_in, short_filter, filter_spectrum, out_grad):
    zs, ys, xs = sizes = tuple(lax.axis_size(a) for a in ("z", "y", "ch"))
    rows, depth = features.shape
    piece, _, width = w_in.shape
    flat = 3 * width
    half = width // 2
    shards, near = zs * ys * 2, ys * 2
    per = half // shards // 2
    message = (2, shards, per, 2 * rows)
    count = out_grad.shape[1] // shards
    dma = pltpu.SemaphoreType.DMA
    vmem = pl.BlockSpec(memory_space=pltpu.VMEM)
    hbm = pl.BlockSpec(memory_space=pl.ANY)
    fixed = [jnp.asarray(t) for t in tables(shards, rows, per)]
    outs = (
        jax.ShapeDtypeStruct((rows, width), BF16),
        jax.ShapeDtypeStruct((count, width), F32),
    )
    results = pl.pallas_call(
        functools.partial(operator_kernel, sizes),
        out_shape=outs,
        in_specs=[hbm] * 8,
        out_specs=(vmem, vmem),
        scratch_shapes=[
            pltpu.VMEM((rows + HALO, depth * xs), BF16),
            pltpu.VMEM((piece * shards, flat), BF16),
            pltpu.VMEM((rows + HALO, flat), F32),
            pltpu.VMEM((rows, width), F32),
            pltpu.VMEM((2, rows, width), F32),
            pltpu.VMEM((shards, 2, 2, per, 2 * rows), BF16),
            pltpu.VMEM((shards, 2, 2, per, 2 * rows), BF16),
            pltpu.VMEM((2, 2, 2 * per * shards, rows), F32),
            pltpu.VMEM((near, rows, zs // 2 * 128), BF16),
            pltpu.VMEM((zs // 2 * 128, near * rows), BF16),
            *[pltpu.VMEM(message, BF16)] * 4,
            pltpu.VMEM((2, near, rows, half), BF16),
            pltpu.VMEM((2, zs // 2, 2 * count, half), BF16),
            pltpu.VMEM((2, 5, count, half), BF16),
            pltpu.VMEM((2, 3, 2 * count, half), BF16),
            *[pltpu.VMEM(t.shape, t.dtype) for t in fixed],
            pltpu.VMEM(short_filter.shape, F32),
            dma((9 + zs // 2,)), dma((2, zs, ys)), dma((2, zs, ys)), dma((zs, ys)), dma((zs, ys)),
            dma((xs - 1,)), dma((xs - 1,)), dma((xs - 1,)), dma((xs - 1,)), dma, dma, dma, dma,
            dma, dma, dma((xs - 1,)), dma((xs - 1,)), dma((2,)), dma((2,)),
            dma((2,)), dma((2,)), dma((2, ys)), dma((2, ys)), dma((2, ys)), dma((2, ys)), dma((2, zs // 2, 2)), dma((2,)),
            dma((2, zs // 2)), dma((2, 3)),
        ],
        compiler_params=pltpu.CompilerParams(
            collective_id=0, has_side_effects=True, vmem_limit_bytes=56 << 20
        ),
        name="operator",
    )(features, w_in.transpose(1, 0, 2), short_filter, filter_spectrum, out_grad, *fixed)
    return pl.pallas_call(
        settle_kernel, out_shape=outs, in_specs=[vmem] * 2, out_specs=(vmem, vmem), name="settle"
    )(*results)


def solution(mesh):
    fine = Mesh(mesh.devices.reshape(8, 4, 2, 4), ("z", "y", "core", "ch"))
    in_specs = (
        P(CTX, "ch"),
        P(CTX, None, "ch"),
        P(None, None, "ch"),
        P(None, CTX, "ch"),
        P(CTX, None),
    )
    out_specs = (P(CTX, "ch"), P(CTX, "ch"))
    return jax.shard_map(
        on_device, mesh=fine, in_specs=in_specs, out_specs=out_specs, check_vma=False
    )
```

```python
import functools
import heapq

import jax
import jax.numpy as jnp
import numpy as np
from jax import lax
from jax.experimental import pallas as pl
from jax.experimental.pallas import tpu as pltpu
from jax.sharding import Mesh, PartitionSpec as P

CTX = ("z", "y", "core")
MESH = pl.DeviceIdType.MESH
HALO = 16
TILE = 256
MATMUL_FROM = 36
FREQ_FROM = 11
GRAD_AT = 1
F32 = jnp.float32
BF16 = jnp.bfloat16


def ring_plan(zs, ys, share):
    z_max, z_min = zs // 2, -((zs - 1) // 2)
    y_max, y_min = ys // 2, -((ys - 1) // 2)
    size = {0: share * 2.1, 1: (1 - share) * 2.1}

    def steps(at, low, high):
        if at == 0:
            return [d for d, ok in ((1, high > 0), (-1, low < 0)) if ok]
        return [1] if 0 < at < high else [-1] if low < at < 0 else []

    def onward(part, fz, fy):
        along_z = [("z", d, (fz + d, fy)) for d in steps(fz, z_min, z_max)]
        along_y = [("y", d, (fz, fy + d)) for d in steps(fy, y_min, y_max)]
        if part == 0:
            return (along_y if fz == 0 else []) + along_z
        return (along_z if fy == 0 else []) + along_y

    free = {"y": 0.0, "z": 0.0}
    order, count = [], 2
    waiting = [(0.0, 0, 1, 0, 0), (0.0, 1, 0, 0, 0)]
    while waiting:
        now, _, part, fz, fy = heapq.heappop(waiting)
        sends = onward(part, fz, fy)
        order.append((part, fz, fy, sends))
        for axis, _, key in sends:
            free[axis] = max(free[axis], now) + size[part]
            count += 1
            heapq.heappush(waiting, (free[axis] + 1.7, count, part, *key))
    return order


def bit_reversed(count):
    bits = count.bit_length() - 1
    return np.array([int(format(i, f"0{bits}b")[::-1], 2) for i in range(count)])


def halves(table):
    high = table.astype(BF16)
    return high, (table - high.astype(np.float64)).astype(BF16)


def tables(shards, rows, per):
    total = shards * rows
    k1 = bit_reversed(shards)
    outer = 2 * np.pi / shards * (np.outer(k1, np.arange(shards)) % shards)
    turn = 2 * np.pi / total * np.outer(k1, np.arange(rows))
    turn = np.tile(np.repeat(turn, per, axis=0), (2, 1))
    inner = 2 * np.pi / rows * (np.outer(np.arange(rows), np.arange(rows)) % rows)
    across = np.kron(np.concatenate([np.cos(outer), -np.sin(outer)]), np.eye(per))
    return (
        np.stack(halves(across)),
        np.stack([np.cos(turn), np.sin(turn)]).astype(np.float32),
        np.stack([*halves(np.cos(inner)), *halves(np.sin(inner))]),
    )


def operator_kernel(
    sizes,
    x_in, w_in, taps_hbm, freq_hbm, grad_hbm, across_hbm, turn_hbm, inner_hbm,
    gated, w_grad,
    x_all, w_all, total, query, freq_in, freq_out, freq_all, freq_wide, grad_all, grad_turned,
    sig_out, sig_all, conv_out, conv_all, gated_all, part_out, part_all, relayed, across, turns, inner, taps,
    local_sem, ring_send, ring_recv, twin_send, twin_recv, x_send, x_recv,
    halo_send, halo_recv, edge_send, edge_recv, freq_send, freq_recv,
    grad_send, grad_recv, grad_x_send, grad_x_recv, sig_send, sig_recv,
    conv_send, conv_recv, gated_send, gated_recv, pair_send, pair_recv, part_send, part_recv, relay_send, relay_recv,
):
    zs, ys, xs = sizes
    rows, depth = x_in.shape
    _, piece, width = w_in.shape
    flat = 3 * width
    half, quarter = width // 2, width // 4
    shards = zs * ys * 2
    near = ys * 2
    first = 5 * flat // 12 // 128 * 128
    z, y, core, x = (lax.axis_index(a) for a in ("z", "y", "core", "ch"))
    turn = 1 - 2 * core
    wrap = lambda v, n: lax.rem(v + 2 * n, n)
    here = (z * ys + y) * 2 + core
    group = y * 2 + core

    def device(place):
        chip = lax.div(place, 2)
        return {"z": lax.div(chip, ys), "y": lax.rem(chip, ys), "core": lax.rem(place, 2), "ch": x}

    def by_axis(axis, step):
        if axis == "z":
            return {"z": wrap(z + turn * step, zs), "y": y, "core": core, "ch": x}
        if axis == "y":
            return {"z": z, "y": wrap(y + turn * step, ys), "core": core, "ch": x}
        return {"z": z, "y": y, "core": core, "ch": lax.rem(x + step, xs)}

    def in_group(other):
        return {"z": z, "y": other // 2, "core": other % 2, "ch": x}

    twin = in_group(y * 2 + 1 - core)
    after, before = lax.rem(here + 1, shards), lax.rem(here + shards - 1, shards)
    peers = [by_axis("z", 1), by_axis("z", -1)]
    peers += [in_group(lax.rem(group + p, near)) for p in range(1, near)]
    peers += [by_axis("ch", d) for d in range(1, xs)] + [device(after), device(before)]
    barrier = pltpu.get_barrier_semaphore()
    for peer in peers:
        pl.semaphore_signal(barrier, inc=1, device_id=peer, device_id_type=MESH)

    z_low, y_low = (zs - 1) // 2, (ys - 1) // 2
    columns = (slice(0, first), slice(first, flat))

    def place_of(fz, fy, of_core):
        zo, yo = wrap(z - turn * fz, zs), wrap(y - turn * fy, ys)
        return (zo * ys + yo) * 2 + of_core

    def slot(fz, fy, of_core):
        return pl.ds(pl.multiple_of(place_of(fz, fy, of_core) * piece, piece), piece)

    def x_rows(of, n, row):
        return x_all.at[pl.ds(row, n), pl.ds(pl.multiple_of(of * depth, depth), depth)]

    share = rows // xs
    mine = pl.ds(pl.multiple_of(share * x, share), share)
    blocks = zs // 2

    def grad_piece(other, k):
        column = ((other % 2 * blocks + k) * ys + other // 2) * 128
        return grad_hbm.at[mine, pl.ds(pl.multiple_of(column, 128), 128)]

    def local(src, dst, n):
        copy = pltpu.make_async_copy(src, dst, local_sem.at[n])
        copy.start()
        return copy

    own_w = [
        local(w_in.at[j], w_all.at[slot(0, 0, core), pl.ds(j * width, width)], 6 + j) for j in range(3)
    ]
    own_x = local(x_in, x_rows(x, rows, HALO), 0)
    load_freq = local(freq_hbm, freq_in, 1)
    loads = [
        local(src, dst, 2 + n)
        for n, (src, dst) in enumerate(((across_hbm, across), (turn_hbm, turns), (inner_hbm, inner), (taps_hbm, taps)))
    ]
    loads += [
        local(grad_piece(group, k), grad_all.at[group, mine, pl.ds(128 * k, 128)], 9 + k)
        for k in range(blocks)
    ]
    for copy in own_w:
        copy.wait()
    pl.semaphore_wait(barrier, len(peers))

    def remote(src, dst, send, recv, to=twin):
        return pltpu.make_async_remote_copy(
            src_ref=src, dst_ref=dst, send_sem=send, recv_sem=recv,
            device_id=to, device_id_type=MESH,
        )

    sends = []

    def start(copy):
        copy.start()
        sends.append(copy)

    def ring_copy(part, origin, key, axis, step):
        where = w_all.at[slot(*origin, core), columns[part]]
        sem = (part, key[0] + z_low, key[1] + y_low)
        return remote(where, where, ring_send.at[sem], ring_recv.at[sem], by_axis(axis, step))

    def open_x():
        own_x.wait()
        start(remote(
            x_rows(x, HALO, rows), x_rows(x, HALO, 0), edge_send, edge_recv, device(after)
        ))
        for d in range(1, xs):
            start(remote(x_rows(x, rows, HALO), x_rows(x, rows, HALO), x_send.at[d - 1], x_recv.at[d - 1], by_axis("ch", d)))

    def send_grad():
        for p in range(1, near):
            other = lax.rem(group + p, near)
            for k in range(blocks):
                remote(
                    grad_piece(other, k), grad_all.at[group, mine, pl.ds(128 * k, 128)],
                    grad_send, grad_recv, in_group(other),
                ).start()

    grad_arrivals = grad_all.at[pl.ds(0, near - 1), pl.ds(0, share)]

    def pass_grad():
        for copy in loads:
            copy.wait()
        remote(grad_arrivals, grad_arrivals, grad_send, grad_recv).wait_recv()
        for d in range(1, xs):
            own = grad_all.at[:, mine]
            start(remote(own, own, grad_x_send.at[d - 1], grad_x_recv.at[d - 1], by_axis("ch", d)))

    def pass_halo():
        remote(x_rows(x, HALO, 0), x_rows(x, HALO, 0), edge_send, edge_recv).wait_recv()
        for d in range(1, xs):
            own = x_rows(x, HALO, 0)
            start(remote(own, own, halo_send.at[d - 1], halo_recv.at[d - 1], by_axis("ch", d)))

    def close_x():
        for n, row, send, recv in ((rows, HALO, x_send, x_recv), (HALO, 0, halo_send, halo_recv)):
            for d in range(1, xs):
                theirs = x_rows(lax.rem(x + xs - d, xs), n, row)
                remote(theirs, theirs, send.at[d - 1], recv.at[d - 1]).wait_recv()

    def turn_freq():
        load_freq.wait()
        for h in range(2):
            for p in range(2):
                stacked = jnp.concatenate(
                    [freq_in[p, :, at : at + quarter] for at in (h * half, h * half + quarter)], axis=0
                )
                freq_out[:, h, p] = stacked.T.astype(BF16).reshape(shards, 2, 2 * rows)
        freq_all[here] = freq_out[here]

    later = []

    def send_freq(*key):
        later.append(key)
        if index >= FREQ_FROM:
            for each in later:
                place = place_of(*each)
                remote(freq_out.at[place], freq_all.at[here], freq_send, freq_recv, device(place)).start()
            later.clear()

    span = near * piece

    def mirror(f, n):
        return f if 2 * f == n else -f

    def meet(fz):
        for fy in range(-y_low, ys // 2 + 1):
            sem = (mirror(fz, zs) + z_low, mirror(fy, ys) + y_low)
            where = w_all.at[slot(fz, fy, 1 - core)]
            remote(where, where, twin_send.at[sem], twin_recv.at[sem]).wait_recv()
            send_freq(fz, fy, 1 - core)

    def multiply(fz, opening, tiles):
        base = pl.multiple_of(wrap(z - turn * fz, zs) * span, span)
        left = x_all[:, pl.ds(base, span)]
        begin, step, count = tiles

        @pl.loop(0, count)
        def _(n):
            cols = pl.ds(pl.multiple_of((begin + step * n) * TILE, TILE), TILE)
            part = jnp.dot(left, w_all[pl.ds(base, span), cols], preferred_element_type=F32)
            if opening:
                total[:, cols] = part
            else:
                total[:, cols] += part

    plan = ring_plan(zs, ys, first / flat)
    arrived, pending, multiplied = set(), [], []
    for index, (part, fz, fy, onward) in enumerate(plan):
        if (fz, fy) != (0, 0):
            sem = (part, fz + z_low, fy + y_low)
            where = w_all.at[slot(fz, fy, core), columns[part]]
            remote(where, where, ring_send.at[sem], ring_recv.at[sem]).wait_recv()
        for axis, step, key in onward:
            start(ring_copy(part, (fz, fy), key, axis, step))
        arrived.add((part, fz, fy))
        if (1 - part, fz, fy) in arrived:
            sem = (fz + z_low, fy + y_low)
            where = w_all.at[slot(fz, fy, core)]
            start(remote(where, where, twin_send.at[sem], twin_recv.at[sem], twin))
            if (fz, fy) != (0, 0):
                send_freq(fz, fy, core)
        if index == 1:
            open_x()
        if index == GRAD_AT:
            send_grad()
        if index == 5:
            pass_halo()
        if index == 11:
            turn_freq()
        pending += sorted(
            (k for k in range(-z_low, zs // 2 + 1) if k not in multiplied and k not in pending
             and all((p, g, f) in arrived for p in (0, 1) for g in (k, mirror(k, zs))
                     for f in range(-y_low, ys // 2 + 1))),
            key=abs,
        )
        if pending and index >= MATMUL_FROM and index % 3 == 0:
            if not multiplied:
                close_x()
                pass_grad()
            multiplied.append(pending.pop(0))
            meet(multiplied[-1])
            multiply(multiplied[-1], len(multiplied) == 1, (0, 1, flat // TILE))
    for fz in pending:
        meet(fz)

    def short(j, at):
        cols = slice(j * width + at, j * width + at + half)
        total[0:HALO, cols] = jnp.where(here == 0, 0.0, total[0:HALO, cols])
        return sum(
            taps[i, j : j + 1, at : at + half]
            * total[HALO - i : HALO - i + rows, cols].astype(BF16).astype(F32)
            for i in range(3)
        )

    def exchange(h, out, into, send, recv):
        @pl.loop(0, shards - 1)
        def _(n):
            to = lax.rem(here + 1 + n, shards)
            remote(out.at[h, to], into.at[h, here], send.at[h], recv.at[h], device(to)).start()

        into[h, here] = out[h, here]

    others = pl.ds(0, shards - 1)

    def arrivals(h, into, send, recv):
        remote(into.at[h, others], into.at[h, others], send.at[h], recv.at[h]).wait_recv()

    for h in range(2):
        for fz in pending:
            multiply(fz, False, (2 + h, 2, 2))
        signal = short(1, h * half) * short(2, h * half)
        stacked = jnp.concatenate([signal[:, :quarter], signal[:, quarter:]], axis=0)
        sig_out[h] = stacked.T.astype(BF16).reshape(shards, 2, 2 * rows)
        exchange(h, sig_out, sig_all, sig_send, sig_recv)
    for fz in pending:
        multiply(fz, False, (0, 1, 2))
    for at in (0, half):
        query[:, at : at + half] = short(0, at)

    lines = 2 * shards
    blocks_of = (slice(0, rows), slice(rows, 2 * rows))
    mul = functools.partial(jnp.dot, preferred_element_type=F32)
    back = lambda a, b: lax.dot_general(a, b, (((0,), (0,)), ((), ())), preferred_element_type=F32)
    join = functools.partial(jnp.concatenate, axis=0)

    def split(value):
        high = value.astype(BF16)
        return high, (value - high.astype(F32)).astype(BF16)

    def within(real, imag):
        high, low = split(join([real, imag]))
        cos = mul(high, inner[0]) + mul(low, inner[0]) + mul(high, inner[1])
        sin = mul(high, inner[2]) + mul(low, inner[2]) + mul(high, inner[3])
        return cos[: 2 * lines], cos[2 * lines :], sin[: 2 * lines], sin[2 * lines :]

    def convolve(h):
        data = [sig_all[h, :, :, u].reshape(lines, rows) for u in blocks_of]
        data = [mul(across[0], d) + mul(across[1], d) for d in data]
        real, imag = join([d[:lines] for d in data]), join([d[lines:] for d in data])
        cos, sin = turns[0], turns[1]
        real_cos, imag_cos, real_sin, imag_sin = within(
            real * cos + imag * sin, imag * cos - real * sin
        )
        real, imag = real_cos + imag_sin, imag_cos - real_sin
        freq_real, freq_imag = freq_wide[h, 0], freq_wide[h, 1]
        real_cos, imag_cos, real_sin, imag_sin = within(
            real * freq_real - imag * freq_imag, real * freq_imag + imag * freq_real
        )
        real, imag = real_cos - imag_sin, imag_cos + real_sin
        real, imag = real * cos - imag * sin, imag * cos + real * sin
        for n, u in enumerate(blocks_of):
            own = slice(n * lines, (n + 1) * lines)
            high, low = split(join([real[own], imag[own]]))
            data = back(across[0], high) + back(across[0], low) + back(across[1], high)
            data = (data * (1 / (shards * rows))).astype(BF16)
            conv_out[h, :, :, u] = data.reshape(shards, 2, rows)
        exchange(h, conv_out, conv_all, conv_send, conv_recv)

    remote(freq_all.at[others], freq_all.at[others], freq_send, freq_recv).wait_recv()
    for h in range(2):
        for p in range(2):
            freq_wide[h, p] = join(
                [freq_all[:, h, p, :, u].reshape(lines, rows).astype(F32) for u in blocks_of]
            )
    for h in range(2):
        arrivals(h, sig_all, sig_send, sig_recv)
        convolve(h)

    def gated_from(h, fy, of_core):
        return gated_all.at[h, wrap(y - turn * fy, ys) * 2 + of_core]

    def pass_gated(h, fy, step):
        block = gated_from(h, fy, core)
        sem = (h, y_low + (ys // 2 if 2 * abs(fy + step) == ys else fy + step))
        start(remote(block, block, gated_send.at[sem], gated_recv.at[sem], by_axis("y", step)))

    def pair_gated(h, fy):
        block, sem = gated_from(h, fy, core), (h, y_low + fy)
        start(remote(block, block, pair_send.at[sem], pair_recv.at[sem], twin))

    def take_gated(h, fy):
        block, sem = gated_from(h, fy, core), (h, y_low + fy)
        remote(block, block, gated_send.at[sem], gated_recv.at[sem]).wait_recv()
        if abs(fy) == 1 and fy == 1 - 2 * h:
            pass_gated(h, fy, fy)
        pair_gated(h, fy)

    def gate(h):
        arrivals(h, conv_all, conv_send, conv_recv)
        conv = conv_all[h].reshape(lines, 2 * rows).astype(F32).T
        for n in range(2):
            at = h * half + n * quarter
            value = query[:, at : at + quarter] * conv[n * rows : (n + 1) * rows]
            gated_all[h, group, :, n * quarter : (n + 1) * quarter] = value.astype(BF16)
        pass_gated(h, 0, 1)
        pass_gated(h, 0, -1)
        pair_gated(h, 0)
        gated[:, h * half : (h + 1) * half] = gated_all[h, group]

    for d in range(1, xs):
        of = lax.rem(x + xs - d, xs)
        theirs = grad_all.at[:, pl.ds(pl.multiple_of(share * of, share), share)]
        remote(theirs, theirs, grad_x_send.at[d - 1], grad_x_recv.at[d - 1]).wait_recv()
    grad_turned[...] = grad_all[...].reshape(near * rows, blocks * 128).T
    count = w_grad.shape[0]

    def distance(h, k):
        return lax.rem((1 - 2 * h) * (z - core * blocks - k) + 2 * zs, zs)

    def relay_copy(h, k, to, n):
        step = z - (1 - 2 * h) * to
        return remote(
            part_out.at[h, k], relayed.at[h, n], relay_send.at[h, k], relay_recv.at[h, n],
            {"z": wrap(step, zs), "y": y, "core": core, "ch": x},
        )

    def final_copy(h, k, c, n):
        return remote(
            part_out.at[h, k, pl.ds(c * count, count)], part_all.at[h, n],
            part_send.at[h, k, c], part_recv.at[h],
            {"z": core * blocks + k, "y": y, "core": c, "ch": x},
        )

    ends = {0: 0, 1: 1, zs - 1: 2, 2: 3, zs - 2: 4}
    relays = {3: (1, 0), 4: (2, 1), zs - 3: (-1, 2)}

    def send_part(h, k, away, act):
        for c in range(2):
            if away:
                act(final_copy(h, k, c, ends[away]))
            else:

                @pl.when(core != c)
                def _():
                    act(final_copy(h, k, c, 0))

    def products(h):
        for fy in range(-y_low, ys // 2 + 1):
            block, sem = gated_from(h, fy, 1 - core), (h, y_low + mirror(fy, ys))
            remote(block, block, pair_send.at[sem], pair_recv.at[sem]).wait_recv()
        right = gated_all[h].reshape(near * rows, half)
        for k in range(blocks):
            part_out[h, k] = mul(grad_turned[128 * k : 128 * (k + 1)], right).astype(BF16)
        for k in range(blocks):
            for away, (to, n) in relays.items():

                @pl.when(distance(h, k) == away)
                def _():
                    relay_copy(h, k, to, n).start()

        for k in range(blocks):
            for away in (1, zs - 1, 0):

                @pl.when(distance(h, k) == away)
                def _():
                    send_part(h, k, away, lambda copy: copy.start())
                    if not away:
                        part_all[h, 0] = part_out[h, k, pl.ds(pl.multiple_of(core * count, count), count)]

    def combine(h):
        for k in range(blocks):
            for away, inputs in ((2, (0, 1)), (zs - 2, (2,))):

                @pl.when(distance(h, k) == away)
                def _():
                    for n in inputs:
                        remote(
                            relayed.at[h, n], relayed.at[h, n], relay_send.at[h, k], relay_recv.at[h, n]
                        ).wait_recv()
                    total_part = part_out[h, k].astype(F32)
                    for n in inputs:
                        total_part += relayed[h, n].astype(F32)
                    part_out[h, k] = total_part.astype(BF16)
                    send_part(h, k, away, lambda copy: copy.start())

    gate(0)
    take_gated(0, 1)
    take_gated(0, -1)
    gate(1)
    take_gated(0, 2)
    products(0)
    take_gated(1, -1)
    take_gated(1, 1)
    combine(0)
    take_gated(1, 2)
    products(1)
    combine(1)
    keeps = core == z // blocks

    def close_parts(h, number):
        some = part_all.at[h, pl.ds(0, number)]
        remote(some, some, part_send.at[h, 0, 0], part_recv.at[h]).wait_recv()

    for h in range(2):

        @pl.when(keeps)
        def _():
            close_parts(h, len(ends) - 1)

        @pl.when(jnp.logical_not(keeps))
        def _():
            close_parts(h, len(ends))

        w_grad[:, h * half : (h + 1) * half] = sum(part_all[h, n].astype(F32) for n in range(len(ends)))
        for k in range(blocks):
            for away in range(zs):

                @pl.when(distance(h, k) == away)
                def _():
                    if away in relays:
                        relay_copy(h, k, *relays[away]).wait_send()
                    else:
                        send_part(h, k, away, lambda copy: copy.wait_send())

    for copy in sends:
        copy.wait_send()
    remote(grad_arrivals, grad_arrivals, grad_send, grad_recv).wait_send()
    remote(freq_all.at[others], freq_all.at[others], freq_send, freq_recv).wait_send()
    for h in range(2):
        for into, send, recv in ((sig_all, sig_send, sig_recv), (conv_all, conv_send, conv_recv)):
            remote(into.at[h, others], into.at[h, others], send.at[h], recv.at[h]).wait_send()


def settle_kernel(a, b, a_out, b_out):
    a_out[...] = a[...]
    b_out[...] = b[...]


def on_device(features, w_in, short_filter, filter_spectrum, out_grad):
    zs, ys, xs = sizes = tuple(lax.axis_size(a) for a in ("z", "y", "ch"))
    rows, depth = features.shape
    piece, _, width = w_in.shape
    flat = 3 * width
    half = width // 2
    shards, near = zs * ys * 2, ys * 2
    per = half // shards // 2
    message = (2, shards, per, 2 * rows)
    count = out_grad.shape[1] // shards
    dma = pltpu.SemaphoreType.DMA
    vmem = pl.BlockSpec(memory_space=pltpu.VMEM)
    hbm = pl.BlockSpec(memory_space=pl.ANY)
    fixed = [jnp.asarray(t) for t in tables(shards, rows, per)]
    outs = (
        jax.ShapeDtypeStruct((rows, width), BF16),
        jax.ShapeDtypeStruct((count, width), F32),
    )
    results = pl.pallas_call(
        functools.partial(operator_kernel, sizes),
        out_shape=outs,
        in_specs=[hbm] * 8,
        out_specs=(vmem, vmem),
        scratch_shapes=[
            pltpu.VMEM((rows + HALO, depth * xs), BF16),
            pltpu.VMEM((piece * shards, flat), BF16),
            pltpu.VMEM((rows + HALO, flat), F32),
            pltpu.VMEM((rows, width), F32),
            pltpu.VMEM((2, rows, width), F32),
            pltpu.VMEM((shards, 2, 2, per, 2 * rows), BF16),
            pltpu.VMEM((shards, 2, 2, per, 2 * rows), BF16),
            pltpu.VMEM((2, 2, 2 * per * shards, rows), F32),
            pltpu.VMEM((near, rows, zs // 2 * 128), BF16),
            pltpu.VMEM((zs // 2 * 128, near * rows), BF16),
            *[pltpu.VMEM(message, BF16)] * 4,
            pltpu.VMEM((2, near, rows, half), BF16),
            pltpu.VMEM((2, zs // 2, 2 * count, half), BF16),
            pltpu.VMEM((2, 5, count, half), BF16),
            pltpu.VMEM((2, 3, 2 * count, half), BF16),
            *[pltpu.VMEM(t.shape, t.dtype) for t in fixed],
            pltpu.VMEM(short_filter.shape, F32),
            dma((9 + zs // 2,)), dma((2, zs, ys)), dma((2, zs, ys)), dma((zs, ys)), dma((zs, ys)),
            dma((xs - 1,)), dma((xs - 1,)), dma((xs - 1,)), dma((xs - 1,)), dma, dma, dma, dma,
            dma, dma, dma((xs - 1,)), dma((xs - 1,)), dma((2,)), dma((2,)),
            dma((2,)), dma((2,)), dma((2, ys)), dma((2, ys)), dma((2, ys)), dma((2, ys)), dma((2, zs // 2, 2)), dma((2,)),
            dma((2, zs // 2)), dma((2, 3)),
        ],
        compiler_params=pltpu.CompilerParams(
            collective_id=0, has_side_effects=True, vmem_limit_bytes=56 << 20
        ),
        name="operator",
    )(features, w_in.transpose(1, 0, 2), short_filter, filter_spectrum, out_grad, *fixed)
    return pl.pallas_call(
        settle_kernel, out_shape=outs, in_specs=[vmem] * 2, out_specs=(vmem, vmem), name="settle"
    )(*results)


def solution(mesh):
    fine = Mesh(mesh.devices.reshape(8, 4, 2, 4), ("z", "y", "core", "ch"))
    in_specs = (
        P(CTX, "ch"),
        P(CTX, None, "ch"),
        P(None, None, "ch"),
        P(None, CTX, "ch"),
        P(CTX, None),
    )
    out_specs = (P(CTX, "ch"), P(CTX, "ch"))
    return jax.shard_map(
        on_device, mesh=fine, in_specs=in_specs, out_specs=out_specs, check_vma=False
    )
```

```python
import functools
import heapq

import jax
import jax.numpy as jnp
import numpy as np
from jax import lax
from jax.experimental import pallas as pl
from jax.experimental.pallas import tpu as pltpu
from jax.sharding import Mesh, PartitionSpec as P

CTX = ("z", "y", "core")
MESH = pl.DeviceIdType.MESH
HALO = 16
TILE = 256
MATMUL_FROM = 36
FREQ_FROM = 11
GRAD_AT = 1
F32 = jnp.float32
BF16 = jnp.bfloat16


def ring_plan(zs, ys, share):
    z_max, z_min = zs // 2, -((zs - 1) // 2)
    y_max, y_min = ys // 2, -((ys - 1) // 2)
    size = {0: share * 2.1, 1: (1 - share) * 2.1}

    def steps(at, low, high):
        if at == 0:
            return [d for d, ok in ((1, high > 0), (-1, low < 0)) if ok]
        return [1] if 0 < at < high else [-1] if low < at < 0 else []

    def onward(part, fz, fy):
        along_z = [("z", d, (fz + d, fy)) for d in steps(fz, z_min, z_max)]
        along_y = [("y", d, (fz, fy + d)) for d in steps(fy, y_min, y_max)]
        if part == 0:
            return (along_y if fz == 0 else []) + along_z
        return (along_z if fy == 0 else []) + along_y

    free = {"y": 0.0, "z": 0.0}
    order, count = [], 2
    waiting = [(0.0, 0, 1, 0, 0), (0.0, 1, 0, 0, 0)]
    while waiting:
        now, _, part, fz, fy = heapq.heappop(waiting)
        sends = onward(part, fz, fy)
        order.append((part, fz, fy, sends))
        for axis, _, key in sends:
            free[axis] = max(free[axis], now) + size[part]
            count += 1
            heapq.heappush(waiting, (free[axis] + 1.7, count, part, *key))
    return order


def bit_reversed(count):
    bits = count.bit_length() - 1
    return np.array([int(format(i, f"0{bits}b")[::-1], 2) for i in range(count)])


def halves(table):
    high = table.astype(BF16)
    return high, (table - high.astype(np.float64)).astype(BF16)


def tables(shards, rows, per):
    total = shards * rows
    k1 = bit_reversed(shards)
    outer = 2 * np.pi / shards * (np.outer(k1, np.arange(shards)) % shards)
    turn = 2 * np.pi / total * np.outer(k1, np.arange(rows))
    turn = np.tile(np.repeat(turn, per, axis=0), (2, 1))
    inner = 2 * np.pi / rows * (np.outer(np.arange(rows), np.arange(rows)) % rows)
    across = np.kron(np.concatenate([np.cos(outer), -np.sin(outer)]), np.eye(per))
    return (
        np.stack(halves(across)),
        np.stack([np.cos(turn), np.sin(turn)]).astype(np.float32),
        np.stack([*halves(np.cos(inner)), *halves(np.sin(inner))]),
    )


def operator_kernel(
    sizes,
    x_in, w_in, taps_hbm, freq_hbm, grad_hbm, across_hbm, turn_hbm, inner_hbm,
    gated, w_grad,
    x_all, w_all, total, query, freq_in, freq_out, freq_all, freq_wide, grad_all, grad_turned,
    sig_out, sig_all, conv_out, conv_all, gated_all, part_out, part_all, relayed, across, turns, inner, taps,
    local_sem, ring_send, ring_recv, twin_send, twin_recv, x_send, x_recv,
    halo_send, halo_recv, edge_send, edge_recv, freq_send, freq_recv,
    grad_send, grad_recv, grad_x_send, grad_x_recv, sig_send, sig_recv,
    conv_send, conv_recv, gated_send, gated_recv, pair_send, pair_recv, part_send, part_recv, relay_send, relay_recv,
):
    zs, ys, xs = sizes
    rows, depth = x_in.shape
    _, piece, width = w_in.shape
    flat = 3 * width
    half, quarter = width // 2, width // 4
    shards = zs * ys * 2
    near = ys * 2
    first = 5 * flat // 12 // 128 * 128
    z, y, core, x = (lax.axis_index(a) for a in ("z", "y", "core", "ch"))
    turn = 1 - 2 * core
    wrap = lambda v, n: lax.rem(v + 2 * n, n)
    here = (z * ys + y) * 2 + core
    group = y * 2 + core

    def device(place):
        chip = lax.div(place, 2)
        return {"z": lax.div(chip, ys), "y": lax.rem(chip, ys), "core": lax.rem(place, 2), "ch": x}

    def by_axis(axis, step):
        if axis == "z":
            return {"z": wrap(z + turn * step, zs), "y": y, "core": core, "ch": x}
        if axis == "y":
            return {"z": z, "y": wrap(y + turn * step, ys), "core": core, "ch": x}
        return {"z": z, "y": y, "core": core, "ch": lax.rem(x + step, xs)}

    def in_group(other):
        return {"z": z, "y": other // 2, "core": other % 2, "ch": x}

    twin = in_group(y * 2 + 1 - core)
    after, before = lax.rem(here + 1, shards), lax.rem(here + shards - 1, shards)
    peers = [by_axis("z", 1), by_axis("z", -1)]
    peers += [in_group(lax.rem(group + p, near)) for p in range(1, near)]
    peers += [by_axis("ch", d) for d in range(1, xs)] + [device(after), device(before)]
    barrier = pltpu.get_barrier_semaphore()
    for peer in peers:
        pl.semaphore_signal(barrier, inc=1, device_id=peer, device_id_type=MESH)

    z_low, y_low = (zs - 1) // 2, (ys - 1) // 2
    columns = (slice(0, first), slice(first, flat))

    def place_of(fz, fy, of_core):
        zo, yo = wrap(z - turn * fz, zs), wrap(y - turn * fy, ys)
        return (zo * ys + yo) * 2 + of_core

    def slot(fz, fy, of_core):
        return pl.ds(pl.multiple_of(place_of(fz, fy, of_core) * piece, piece), piece)

    def x_rows(of, n, row):
        return x_all.at[pl.ds(row, n), pl.ds(pl.multiple_of(of * depth, depth), depth)]

    share = rows // xs
    mine = pl.ds(pl.multiple_of(share * x, share), share)
    blocks = zs // 2

    def grad_piece(other, k):
        column = ((other % 2 * blocks + k) * ys + other // 2) * 128
        return grad_hbm.at[mine, pl.ds(pl.multiple_of(column, 128), 128)]

    def local(src, dst, n):
        copy = pltpu.make_async_copy(src, dst, local_sem.at[n])
        copy.start()
        return copy

    own_w = [
        local(w_in.at[j], w_all.at[slot(0, 0, core), pl.ds(j * width, width)], 6 + j) for j in range(3)
    ]
    own_x = local(x_in, x_rows(x, rows, HALO), 0)
    load_freq = local(freq_hbm, freq_in, 1)
    loads = [
        local(src, dst, 2 + n)
        for n, (src, dst) in enumerate(((across_hbm, across), (turn_hbm, turns), (inner_hbm, inner), (taps_hbm, taps)))
    ]
    loads += [
        local(grad_piece(group, k), grad_all.at[group, mine, pl.ds(128 * k, 128)], 9 + k)
        for k in range(blocks)
    ]
    for copy in own_w:
        copy.wait()
    pl.semaphore_wait(barrier, len(peers))

    def remote(src, dst, send, recv, to=twin):
        return pltpu.make_async_remote_copy(
            src_ref=src, dst_ref=dst, send_sem=send, recv_sem=recv,
            device_id=to, device_id_type=MESH,
        )

    sends = []

    def start(copy):
        copy.start()
        sends.append(copy)

    def ring_copy(part, origin, key, axis, step):
        where = w_all.at[slot(*origin, core), columns[part]]
        sem = (part, key[0] + z_low, key[1] + y_low)
        return remote(where, where, ring_send.at[sem], ring_recv.at[sem], by_axis(axis, step))

    def open_x():
        own_x.wait()
        start(remote(
            x_rows(x, HALO, rows), x_rows(x, HALO, 0), edge_send, edge_recv, device(after)
        ))
        for d in range(1, xs):
            start(remote(x_rows(x, rows, HALO), x_rows(x, rows, HALO), x_send.at[d - 1], x_recv.at[d - 1], by_axis("ch", d)))

    def send_grad():
        for p in range(1, near):
            other = lax.rem(group + p, near)
            for k in range(blocks):
                remote(
                    grad_piece(other, k), grad_all.at[group, mine, pl.ds(128 * k, 128)],
                    grad_send, grad_recv, in_group(other),
                ).start()

    grad_arrivals = grad_all.at[pl.ds(0, near - 1), pl.ds(0, share)]

    def pass_grad():
        for copy in loads:
            copy.wait()
        remote(grad_arrivals, grad_arrivals, grad_send, grad_recv).wait_recv()
        for d in range(1, xs):
            own = grad_all.at[:, mine]
            start(remote(own, own, grad_x_send.at[d - 1], grad_x_recv.at[d - 1], by_axis("ch", d)))

    def pass_halo():
        remote(x_rows(x, HALO, 0), x_rows(x, HALO, 0), edge_send, edge_recv).wait_recv()
        for d in range(1, xs):
            own = x_rows(x, HALO, 0)
            start(remote(own, own, halo_send.at[d - 1], halo_recv.at[d - 1], by_axis("ch", d)))

    def close_x():
        for n, row, send, recv in ((rows, HALO, x_send, x_recv), (HALO, 0, halo_send, halo_recv)):
            for d in range(1, xs):
                theirs = x_rows(lax.rem(x + xs - d, xs), n, row)
                remote(theirs, theirs, send.at[d - 1], recv.at[d - 1]).wait_recv()

    def turn_freq():
        load_freq.wait()
        for h in range(2):
            for p in range(2):
                stacked = jnp.concatenate(
                    [freq_in[p, :, at : at + quarter] for at in (h * half, h * half + quarter)], axis=0
                )
                freq_out[:, h, p] = stacked.T.astype(BF16).reshape(shards, 2, 2 * rows)
        freq_all[here] = freq_out[here]

    later = []

    def send_freq(*key):
        later.append(key)
        if index >= FREQ_FROM:
            for each in later:
                place = place_of(*each)
                remote(freq_out.at[place], freq_all.at[here], freq_send, freq_recv, device(place)).start()
            later.clear()

    span = near * piece

    def mirror(f, n):
        return f if 2 * f == n else -f

    def meet(fz):
        for fy in range(-y_low, ys // 2 + 1):
            sem = (mirror(fz, zs) + z_low, mirror(fy, ys) + y_low)
            where = w_all.at[slot(fz, fy, 1 - core)]
            remote(where, where, twin_send.at[sem], twin_recv.at[sem]).wait_recv()
            send_freq(fz, fy, 1 - core)

    def multiply(fz, opening, tiles):
        base = pl.multiple_of(wrap(z - turn * fz, zs) * span, span)
        left = x_all[:, pl.ds(base, span)]
        begin, step, count = tiles

        @pl.loop(0, count)
        def _(n):
            cols = pl.ds(pl.multiple_of((begin + step * n) * TILE, TILE), TILE)
            part = jnp.dot(left, w_all[pl.ds(base, span), cols], preferred_element_type=F32)
            if opening:
                total[:, cols] = part
            else:
                total[:, cols] += part

    plan = ring_plan(zs, ys, first / flat)
    arrived, pending, multiplied = set(), [], []
    for index, (part, fz, fy, onward) in enumerate(plan):
        if (fz, fy) != (0, 0):
            sem = (part, fz + z_low, fy + y_low)
            where = w_all.at[slot(fz, fy, core), columns[part]]
            remote(where, where, ring_send.at[sem], ring_recv.at[sem]).wait_recv()
        for axis, step, key in onward:
            start(ring_copy(part, (fz, fy), key, axis, step))
        arrived.add((part, fz, fy))
        if (1 - part, fz, fy) in arrived:
            sem = (fz + z_low, fy + y_low)
            where = w_all.at[slot(fz, fy, core)]
            start(remote(where, where, twin_send.at[sem], twin_recv.at[sem], twin))
            if (fz, fy) != (0, 0):
                send_freq(fz, fy, core)
        if index == 1:
            open_x()
        if index == GRAD_AT:
            send_grad()
        if index == 5:
            pass_halo()
        if index == 11:
            turn_freq()
        pending += sorted(
            (k for k in range(-z_low, zs // 2 + 1) if k not in multiplied and k not in pending
             and all((p, g, f) in arrived for p in (0, 1) for g in (k, mirror(k, zs))
                     for f in range(-y_low, ys // 2 + 1))),
            key=abs,
        )
        if pending and index >= MATMUL_FROM and index % 3 == 0:
            if not multiplied:
                close_x()
                pass_grad()
            multiplied.append(pending.pop(0))
            meet(multiplied[-1])
            multiply(multiplied[-1], len(multiplied) == 1, (0, 1, flat // TILE))
    for fz in pending:
        meet(fz)

    def short(j, at):
        cols = slice(j * width + at, j * width + at + half)
        total[0:HALO, cols] = jnp.where(here == 0, 0.0, total[0:HALO, cols])
        return sum(
            taps[i, j : j + 1, at : at + half]
            * total[HALO - i : HALO - i + rows, cols].astype(BF16).astype(F32)
            for i in range(3)
        )

    def exchange(h, out, into, send, recv):
        @pl.loop(0, shards - 1)
        def _(n):
            to = lax.rem(here + 1 + n, shards)
            remote(out.at[h, to], into.at[h, here], send.at[h], recv.at[h], device(to)).start()

        into[h, here] = out[h, here]

    others = pl.ds(0, shards - 1)

    def arrivals(h, into, send, recv):
        remote(into.at[h, others], into.at[h, others], send.at[h], recv.at[h]).wait_recv()

    for h in range(2):
        for fz in pending:
            multiply(fz, False, (2 + h, 2, 2))
        signal = short(1, h * half) * short(2, h * half)
        stacked = jnp.concatenate([signal[:, :quarter], signal[:, quarter:]], axis=0)
        sig_out[h] = stacked.T.astype(BF16).reshape(shards, 2, 2 * rows)
        exchange(h, sig_out, sig_all, sig_send, sig_recv)
    for fz in pending:
        multiply(fz, False, (0, 1, 2))
    for at in (0, half):
        query[:, at : at + half] = short(0, at)

    lines = 2 * shards
    blocks_of = (slice(0, rows), slice(rows, 2 * rows))
    mul = functools.partial(jnp.dot, preferred_element_type=F32)
    back = lambda a, b: lax.dot_general(a, b, (((0,), (0,)), ((), ())), preferred_element_type=F32)
    join = functools.partial(jnp.concatenate, axis=0)

    def split(value):
        high = value.astype(BF16)
        return high, (value - high.astype(F32)).astype(BF16)

    def within(real, imag):
        high, low = split(join([real, imag]))
        cos = mul(high, inner[0]) + mul(low, inner[0]) + mul(high, inner[1])
        sin = mul(high, inner[2]) + mul(low, inner[2]) + mul(high, inner[3])
        return cos[: 2 * lines], cos[2 * lines :], sin[: 2 * lines], sin[2 * lines :]

    def convolve(h):
        data = [sig_all[h, :, :, u].reshape(lines, rows) for u in blocks_of]
        data = [mul(across[0], d) + mul(across[1], d) for d in data]
        real, imag = join([d[:lines] for d in data]), join([d[lines:] for d in data])
        cos, sin = turns[0], turns[1]
        real_cos, imag_cos, real_sin, imag_sin = within(
            real * cos + imag * sin, imag * cos - real * sin
        )
        real, imag = real_cos + imag_sin, imag_cos - real_sin
        freq_real, freq_imag = freq_wide[h, 0], freq_wide[h, 1]
        real_cos, imag_cos, real_sin, imag_sin = within(
            real * freq_real - imag * freq_imag, real * freq_imag + imag * freq_real
        )
        real, imag = real_cos - imag_sin, imag_cos + real_sin
        real, imag = real * cos - imag * sin, imag * cos + real * sin
        for n, u in enumerate(blocks_of):
            own = slice(n * lines, (n + 1) * lines)
            high, low = split(join([real[own], imag[own]]))
            data = back(across[0], high) + back(across[0], low) + back(across[1], high)
            data = (data * (1 / (shards * rows))).astype(BF16)
            conv_out[h, :, :, u] = data.reshape(shards, 2, rows)
        exchange(h, conv_out, conv_all, conv_send, conv_recv)

    remote(freq_all.at[others], freq_all.at[others], freq_send, freq_recv).wait_recv()
    for h in range(2):
        for p in range(2):
            freq_wide[h, p] = join(
                [freq_all[:, h, p, :, u].reshape(lines, rows).astype(F32) for u in blocks_of]
            )
    for h in range(2):
        arrivals(h, sig_all, sig_send, sig_recv)
        convolve(h)

    def gated_from(h, fy, of_core):
        return gated_all.at[h, wrap(y - turn * fy, ys) * 2 + of_core]

    def pass_gated(h, fy, step):
        block = gated_from(h, fy, core)
        sem = (h, y_low + (ys // 2 if 2 * abs(fy + step) == ys else fy + step))
        start(remote(block, block, gated_send.at[sem], gated_recv.at[sem], by_axis("y", step)))

    def pair_gated(h, fy):
        block, sem = gated_from(h, fy, core), (h, y_low + fy)
        start(remote(block, block, pair_send.at[sem], pair_recv.at[sem], twin))

    def take_gated(h, fy):
        block, sem = gated_from(h, fy, core), (h, y_low + fy)
        remote(block, block, gated_send.at[sem], gated_recv.at[sem]).wait_recv()
        if abs(fy) == 1 and fy == 1 - 2 * h:
            pass_gated(h, fy, fy)
        pair_gated(h, fy)

    def gate(h):
        arrivals(h, conv_all, conv_send, conv_recv)
        conv = conv_all[h].reshape(lines, 2 * rows).astype(F32).T
        for n in range(2):
            at = h * half + n * quarter
            value = query[:, at : at + quarter] * conv[n * rows : (n + 1) * rows]
            gated_all[h, group, :, n * quarter : (n + 1) * quarter] = value.astype(BF16)
        pass_gated(h, 0, 1)
        pass_gated(h, 0, -1)
        pair_gated(h, 0)
        gated[:, h * half : (h + 1) * half] = gated_all[h, group]

    for d in range(1, xs):
        of = lax.rem(x + xs - d, xs)
        theirs = grad_all.at[:, pl.ds(pl.multiple_of(share * of, share), share)]
        remote(theirs, theirs, grad_x_send.at[d - 1], grad_x_recv.at[d - 1]).wait_recv()
    grad_turned[...] = grad_all[...].reshape(near * rows, blocks * 128).T
    count = w_grad.shape[0]

    def distance(h, k):
        return lax.rem((1 - 2 * h) * (z - core * blocks - k) + 2 * zs, zs)

    def relay_copy(h, k, to, n):
        step = z - (1 - 2 * h) * to
        return remote(
            part_out.at[h, k], relayed.at[h, n], relay_send.at[h, k], relay_recv.at[h, n],
            {"z": wrap(step, zs), "y": y, "core": core, "ch": x},
        )

    def final_copy(h, k, c, n):
        return remote(
            part_out.at[h, k, pl.ds(c * count, count)], part_all.at[h, n],
            part_send.at[h, k, c], part_recv.at[h],
            {"z": core * blocks + k, "y": y, "core": c, "ch": x},
        )

    ends = {0: 0, 1: 1, zs - 1: 2, 2: 3, zs - 2: 4}
    relays = {3: (1, 0), 4: (2, 1), zs - 3: (-1, 2)}

    def send_part(h, k, away, act):
        for c in range(2):
            if away:
                act(final_copy(h, k, c, ends[away]))
            else:

                @pl.when(core != c)
                def _():
                    act(final_copy(h, k, c, 0))

    def products(h):
        for fy in range(-y_low, ys // 2 + 1):
            block, sem = gated_from(h, fy, 1 - core), (h, y_low + mirror(fy, ys))
            remote(block, block, pair_send.at[sem], pair_recv.at[sem]).wait_recv()
        right = gated_all[h].reshape(near * rows, half)
        for k in range(blocks):
            part_out[h, k] = mul(grad_turned[128 * k : 128 * (k + 1)], right).astype(BF16)
        for k in range(blocks):
            for away, (to, n) in relays.items():

                @pl.when(distance(h, k) == away)
                def _():
                    relay_copy(h, k, to, n).start()

        for k in range(blocks):
            for away in (1, zs - 1, 0):

                @pl.when(distance(h, k) == away)
                def _():
                    send_part(h, k, away, lambda copy: copy.start())
                    if not away:
                        part_all[h, 0] = part_out[h, k, pl.ds(pl.multiple_of(core * count, count), count)]

    def combine(h):
        for k in range(blocks):
            for away, inputs in ((2, (0, 1)), (zs - 2, (2,))):

                @pl.when(distance(h, k) == away)
                def _():
                    for n in inputs:
                        remote(
                            relayed.at[h, n], relayed.at[h, n], relay_send.at[h, k], relay_recv.at[h, n]
                        ).wait_recv()
                    total_part = part_out[h, k].astype(F32)
                    for n in inputs:
                        total_part += relayed[h, n].astype(F32)
                    part_out[h, k] = total_part.astype(BF16)
                    send_part(h, k, away, lambda copy: copy.start())

    gate(0)
    gate(1)
    take_gated(0, 1)
    take_gated(1, -1)
    take_gated(0, -1)
    take_gated(1, 1)
    take_gated(0, 2)
    products(0)
    take_gated(1, 2)
    products(1)
    combine(0)
    combine(1)
    keeps = core == z // blocks

    def close_parts(h, number):
        some = part_all.at[h, pl.ds(0, number)]
        remote(some, some, part_send.at[h, 0, 0], part_recv.at[h]).wait_recv()

    for h in range(2):

        @pl.when(keeps)
        def _():
            close_parts(h, len(ends) - 1)

        @pl.when(jnp.logical_not(keeps))
        def _():
            close_parts(h, len(ends))

        w_grad[:, h * half : (h + 1) * half] = sum(part_all[h, n].astype(F32) for n in range(len(ends)))
        for k in range(blocks):
            for away in range(zs):

                @pl.when(distance(h, k) == away)
                def _():
                    if away in relays:
                        relay_copy(h, k, *relays[away]).wait_send()
                    else:
                        send_part(h, k, away, lambda copy: copy.wait_send())

    for copy in sends:
        copy.wait_send()
    remote(grad_arrivals, grad_arrivals, grad_send, grad_recv).wait_send()
    remote(freq_all.at[others], freq_all.at[others], freq_send, freq_recv).wait_send()
    for h in range(2):
        for into, send, recv in ((sig_all, sig_send, sig_recv), (conv_all, conv_send, conv_recv)):
            remote(into.at[h, others], into.at[h, others], send.at[h], recv.at[h]).wait_send()


def settle_kernel(a, b, a_out, b_out):
    a_out[...] = a[...]
    b_out[...] = b[...]


def on_device(features, w_in, short_filter, filter_spectrum, out_grad):
    zs, ys, xs = sizes = tuple(lax.axis_size(a) for a in ("z", "y", "ch"))
    rows, depth = features.shape
    piece, _, width = w_in.shape
    flat = 3 * width
    half = width // 2
    shards, near = zs * ys * 2, ys * 2
    per = half // shards // 2
    message = (2, shards, per, 2 * rows)
    count = out_grad.shape[1] // shards
    dma = pltpu.SemaphoreType.DMA
    vmem = pl.BlockSpec(memory_space=pltpu.VMEM)
    hbm = pl.BlockSpec(memory_space=pl.ANY)
    fixed = [jnp.asarray(t) for t in tables(shards, rows, per)]
    outs = (
        jax.ShapeDtypeStruct((rows, width), BF16),
        jax.ShapeDtypeStruct((count, width), F32),
    )
    results = pl.pallas_call(
        functools.partial(operator_kernel, sizes),
        out_shape=outs,
        in_specs=[hbm] * 8,
        out_specs=(vmem, vmem),
        scratch_shapes=[
            pltpu.VMEM((rows + HALO, depth * xs), BF16),
            pltpu.VMEM((piece * shards, flat), BF16),
            pltpu.VMEM((rows + HALO, flat), F32),
            pltpu.VMEM((rows, width), F32),
            pltpu.VMEM((2, rows, width), F32),
            pltpu.VMEM((shards, 2, 2, per, 2 * rows), BF16),
            pltpu.VMEM((shards, 2, 2, per, 2 * rows), BF16),
            pltpu.VMEM((2, 2, 2 * per * shards, rows), F32),
            pltpu.VMEM((near, rows, zs // 2 * 128), BF16),
            pltpu.VMEM((zs // 2 * 128, near * rows), BF16),
            *[pltpu.VMEM(message, BF16)] * 4,
            pltpu.VMEM((2, near, rows, half), BF16),
            pltpu.VMEM((2, zs // 2, 2 * count, half), BF16),
            pltpu.VMEM((2, 5, count, half), BF16),
            pltpu.VMEM((2, 3, 2 * count, half), BF16),
            *[pltpu.VMEM(t.shape, t.dtype) for t in fixed],
            pltpu.VMEM(short_filter.shape, F32),
            dma((9 + zs // 2,)), dma((2, zs, ys)), dma((2, zs, ys)), dma((zs, ys)), dma((zs, ys)),
            dma((xs - 1,)), dma((xs - 1,)), dma((xs - 1,)), dma((xs - 1,)), dma, dma, dma, dma,
            dma, dma, dma((xs - 1,)), dma((xs - 1,)), dma((2,)), dma((2,)),
            dma((2,)), dma((2,)), dma((2, ys)), dma((2, ys)), dma((2, ys)), dma((2, ys)), dma((2, zs // 2, 2)), dma((2,)),
            dma((2, zs // 2)), dma((2, 3)),
        ],
        compiler_params=pltpu.CompilerParams(
            collective_id=0, has_side_effects=True, vmem_limit_bytes=56 << 20
        ),
        name="operator",
    )(features, w_in.transpose(1, 0, 2), short_filter, filter_spectrum, out_grad, *fixed)
    return pl.pallas_call(
        settle_kernel, out_shape=outs, in_specs=[vmem] * 2, out_specs=(vmem, vmem), name="settle"
    )(*results)


def solution(mesh):
    fine = Mesh(mesh.devices.reshape(8, 4, 2, 4), ("z", "y", "core", "ch"))
    in_specs = (
        P(CTX, "ch"),
        P(CTX, None, "ch"),
        P(None, None, "ch"),
        P(None, CTX, "ch"),
        P(CTX, None),
    )
    out_specs = (P(CTX, "ch"), P(CTX, "ch"))
    return jax.shard_map(
        on_device, mesh=fine, in_specs=in_specs, out_specs=out_specs, check_vma=False
    )
```

```python
import functools
import heapq

import jax
import jax.numpy as jnp
import numpy as np
from jax import lax
from jax.experimental import pallas as pl
from jax.experimental.pallas import tpu as pltpu
from jax.sharding import Mesh, PartitionSpec as P

CTX = ("z", "y", "core")
MESH = pl.DeviceIdType.MESH
HALO = 16
TILE = 256
MATMUL_FROM = 36
FREQ_FROM = 11
GRAD_AT = 1
F32 = jnp.float32
BF16 = jnp.bfloat16


def ring_plan(zs, ys, share):
    z_max, z_min = zs // 2, -((zs - 1) // 2)
    y_max, y_min = ys // 2, -((ys - 1) // 2)
    size = {0: share * 2.1, 1: (1 - share) * 2.1}

    def steps(at, low, high):
        if at == 0:
            return [d for d, ok in ((1, high > 0), (-1, low < 0)) if ok]
        return [1] if 0 < at < high else [-1] if low < at < 0 else []

    def onward(part, fz, fy):
        along_z = [("z", d, (fz + d, fy)) for d in steps(fz, z_min, z_max)]
        along_y = [("y", d, (fz, fy + d)) for d in steps(fy, y_min, y_max)]
        if part == 0:
            return (along_y if fz == 0 else []) + along_z
        return (along_z if fy == 0 else []) + along_y

    free = {"y": 0.0, "z": 0.0}
    order, count = [], 2
    waiting = [(0.0, 0, 1, 0, 0), (0.0, 1, 0, 0, 0)]
    while waiting:
        now, _, part, fz, fy = heapq.heappop(waiting)
        sends = onward(part, fz, fy)
        order.append((part, fz, fy, sends))
        for axis, _, key in sends:
            free[axis] = max(free[axis], now) + size[part]
            count += 1
            heapq.heappush(waiting, (free[axis] + 1.7, count, part, *key))
    return order


def bit_reversed(count):
    bits = count.bit_length() - 1
    return np.array([int(format(i, f"0{bits}b")[::-1], 2) for i in range(count)])


def halves(table):
    high = table.astype(BF16)
    return high, (table - high.astype(np.float64)).astype(BF16)


def tables(shards, rows, per):
    total = shards * rows
    k1 = bit_reversed(shards)
    outer = 2 * np.pi / shards * (np.outer(k1, np.arange(shards)) % shards)
    turn = 2 * np.pi / total * np.outer(k1, np.arange(rows))
    turn = np.tile(np.repeat(turn, per, axis=0), (2, 1))
    inner = 2 * np.pi / rows * (np.outer(np.arange(rows), np.arange(rows)) % rows)
    across = np.kron(np.concatenate([np.cos(outer), -np.sin(outer)]), np.eye(per))
    return (
        np.stack(halves(across)),
        np.stack([np.cos(turn), np.sin(turn)]).astype(np.float32),
        np.stack([*halves(np.cos(inner)), *halves(np.sin(inner))]),
    )


def operator_kernel(
    sizes,
    x_in, w_in, taps_hbm, freq_hbm, grad_hbm, across_hbm, turn_hbm, inner_hbm,
    gated, w_grad,
    x_all, w_all, total, query, freq_in, freq_out, freq_all, freq_wide, grad_all, grad_turned,
    sig_out, sig_all, conv_out, conv_all, gated_all, part_out, part_all, relayed, across, turns, inner, taps,
    local_sem, ring_send, ring_recv, twin_send, twin_recv, x_send, x_recv,
    halo_send, halo_recv, edge_send, edge_recv, freq_send, freq_recv,
    grad_send, grad_recv, grad_x_send, grad_x_recv, sig_send, sig_recv,
    conv_send, conv_recv, gated_send, gated_recv, pair_send, pair_recv, part_send, part_recv, relay_send, relay_recv,
):
    zs, ys, xs = sizes
    rows, depth = x_in.shape
    _, piece, width = w_in.shape
    flat = 3 * width
    half, quarter = width // 2, width // 4
    shards = zs * ys * 2
    near = ys * 2
    first = 5 * flat // 12 // 128 * 128
    z, y, core, x = (lax.axis_index(a) for a in ("z", "y", "core", "ch"))
    turn = 1 - 2 * core
    wrap = lambda v, n: lax.rem(v + 2 * n, n)
    here = (z * ys + y) * 2 + core
    group = y * 2 + core

    def device(place):
        chip = lax.div(place, 2)
        return {"z": lax.div(chip, ys), "y": lax.rem(chip, ys), "core": lax.rem(place, 2), "ch": x}

    def by_axis(axis, step):
        if axis == "z":
            return {"z": wrap(z + turn * step, zs), "y": y, "core": core, "ch": x}
        if axis == "y":
            return {"z": z, "y": wrap(y + turn * step, ys), "core": core, "ch": x}
        return {"z": z, "y": y, "core": core, "ch": lax.rem(x + step, xs)}

    def in_group(other):
        return {"z": z, "y": other // 2, "core": other % 2, "ch": x}

    twin = in_group(y * 2 + 1 - core)
    after, before = lax.rem(here + 1, shards), lax.rem(here + shards - 1, shards)
    peers = [by_axis("z", 1), by_axis("z", -1)]
    peers += [in_group(lax.rem(group + p, near)) for p in range(1, near)]
    peers += [by_axis("ch", d) for d in range(1, xs)] + [device(after), device(before)]
    barrier = pltpu.get_barrier_semaphore()
    for peer in peers:
        pl.semaphore_signal(barrier, inc=1, device_id=peer, device_id_type=MESH)

    z_low, y_low = (zs - 1) // 2, (ys - 1) // 2
    columns = (slice(0, first), slice(first, flat))

    def place_of(fz, fy, of_core):
        zo, yo = wrap(z - turn * fz, zs), wrap(y - turn * fy, ys)
        return (zo * ys + yo) * 2 + of_core

    def slot(fz, fy, of_core):
        return pl.ds(pl.multiple_of(place_of(fz, fy, of_core) * piece, piece), piece)

    def x_rows(of, n, row):
        return x_all.at[pl.ds(row, n), pl.ds(pl.multiple_of(of * depth, depth), depth)]

    share = rows // xs
    mine = pl.ds(pl.multiple_of(share * x, share), share)
    blocks = zs // 2

    def grad_piece(other, k):
        column = ((other % 2 * blocks + k) * ys + other // 2) * 128
        return grad_hbm.at[mine, pl.ds(pl.multiple_of(column, 128), 128)]

    def local(src, dst, n):
        copy = pltpu.make_async_copy(src, dst, local_sem.at[n])
        copy.start()
        return copy

    own_w = [
        local(w_in.at[j], w_all.at[slot(0, 0, core), pl.ds(j * width, width)], 6 + j) for j in range(3)
    ]
    own_x = local(x_in, x_rows(x, rows, HALO), 0)
    load_freq = local(freq_hbm, freq_in, 1)
    loads = [
        local(src, dst, 2 + n)
        for n, (src, dst) in enumerate(((across_hbm, across), (turn_hbm, turns), (inner_hbm, inner), (taps_hbm, taps)))
    ]
    loads += [
        local(grad_piece(group, k), grad_all.at[group, mine, pl.ds(128 * k, 128)], 9 + k)
        for k in range(blocks)
    ]
    for copy in own_w:
        copy.wait()
    pl.semaphore_wait(barrier, len(peers))

    def remote(src, dst, send, recv, to=twin):
        return pltpu.make_async_remote_copy(
            src_ref=src, dst_ref=dst, send_sem=send, recv_sem=recv,
            device_id=to, device_id_type=MESH,
        )

    sends = []

    def start(copy):
        copy.start()
        sends.append(copy)

    def ring_copy(part, origin, key, axis, step):
        where = w_all.at[slot(*origin, core), columns[part]]
        sem = (part, key[0] + z_low, key[1] + y_low)
        return remote(where, where, ring_send.at[sem], ring_recv.at[sem], by_axis(axis, step))

    def open_x():
        own_x.wait()
        start(remote(
            x_rows(x, HALO, rows), x_rows(x, HALO, 0), edge_send, edge_recv, device(after)
        ))
        for d in range(1, xs):
            start(remote(x_rows(x, rows, HALO), x_rows(x, rows, HALO), x_send.at[d - 1], x_recv.at[d - 1], by_axis("ch", d)))

    def send_grad():
        for p in range(1, near):
            other = lax.rem(group + p, near)
            for k in range(blocks):
                remote(
                    grad_piece(other, k), grad_all.at[group, mine, pl.ds(128 * k, 128)],
                    grad_send, grad_recv, in_group(other),
                ).start()

    grad_arrivals = grad_all.at[pl.ds(0, near - 1), pl.ds(0, share)]

    def pass_grad():
        for copy in loads:
            copy.wait()
        remote(grad_arrivals, grad_arrivals, grad_send, grad_recv).wait_recv()
        for d in range(1, xs):
            own = grad_all.at[:, mine]
            start(remote(own, own, grad_x_send.at[d - 1], grad_x_recv.at[d - 1], by_axis("ch", d)))

    def pass_halo():
        remote(x_rows(x, HALO, 0), x_rows(x, HALO, 0), edge_send, edge_recv).wait_recv()
        for d in range(1, xs):
            own = x_rows(x, HALO, 0)
            start(remote(own, own, halo_send.at[d - 1], halo_recv.at[d - 1], by_axis("ch", d)))

    def close_x():
        for n, row, send, recv in ((rows, HALO, x_send, x_recv), (HALO, 0, halo_send, halo_recv)):
            for d in range(1, xs):
                theirs = x_rows(lax.rem(x + xs - d, xs), n, row)
                remote(theirs, theirs, send.at[d - 1], recv.at[d - 1]).wait_recv()

    def turn_freq():
        load_freq.wait()
        for h in range(2):
            for p in range(2):
                stacked = jnp.concatenate(
                    [freq_in[p, :, at : at + quarter] for at in (h * half, h * half + quarter)], axis=0
                )
                freq_out[:, h, p] = stacked.T.astype(BF16).reshape(shards, 2, 2 * rows)
        freq_all[here] = freq_out[here]

    later = []

    def send_freq(*key):
        later.append(key)
        if index >= FREQ_FROM:
            for each in later:
                place = place_of(*each)
                remote(freq_out.at[place], freq_all.at[here], freq_send, freq_recv, device(place)).start()
            later.clear()

    span = near * piece

    def mirror(f, n):
        return f if 2 * f == n else -f

    def meet(fz):
        for fy in range(-y_low, ys // 2 + 1):
            sem = (mirror(fz, zs) + z_low, mirror(fy, ys) + y_low)
            where = w_all.at[slot(fz, fy, 1 - core)]
            remote(where, where, twin_send.at[sem], twin_recv.at[sem]).wait_recv()
            send_freq(fz, fy, 1 - core)

    def multiply(fz, opening, tiles):
        base = pl.multiple_of(wrap(z - turn * fz, zs) * span, span)
        left = x_all[:, pl.ds(base, span)]
        begin, step, count = tiles

        @pl.loop(0, count)
        def _(n):
            cols = pl.ds(pl.multiple_of((begin + step * n) * TILE, TILE), TILE)
            part = jnp.dot(left, w_all[pl.ds(base, span), cols], preferred_element_type=F32)
            if opening:
                total[:, cols] = part
            else:
                total[:, cols] += part

    plan = ring_plan(zs, ys, first / flat)
    arrived, pending, multiplied = set(), [], []
    for index, (part, fz, fy, onward) in enumerate(plan):
        if (fz, fy) != (0, 0):
            sem = (part, fz + z_low, fy + y_low)
            where = w_all.at[slot(fz, fy, core), columns[part]]
            remote(where, where, ring_send.at[sem], ring_recv.at[sem]).wait_recv()
        for axis, step, key in onward:
            start(ring_copy(part, (fz, fy), key, axis, step))
        arrived.add((part, fz, fy))
        if (1 - part, fz, fy) in arrived:
            sem = (fz + z_low, fy + y_low)
            where = w_all.at[slot(fz, fy, core)]
            start(remote(where, where, twin_send.at[sem], twin_recv.at[sem], twin))
            if (fz, fy) != (0, 0):
                send_freq(fz, fy, core)
        if index == 1:
            open_x()
        if index == GRAD_AT:
            send_grad()
        if index == 5:
            pass_halo()
        if index == 11:
            turn_freq()
        pending += sorted(
            (k for k in range(-z_low, zs // 2 + 1) if k not in multiplied and k not in pending
             and all((p, g, f) in arrived for p in (0, 1) for g in (k, mirror(k, zs))
                     for f in range(-y_low, ys // 2 + 1))),
            key=abs,
        )
        if pending and index >= MATMUL_FROM and index % 3 == 0:
            if not multiplied:
                close_x()
                pass_grad()
            multiplied.append(pending.pop(0))
            meet(multiplied[-1])
            multiply(multiplied[-1], len(multiplied) == 1, (0, 1, flat // TILE))
    for fz in pending:
        meet(fz)

    def short(j, at):
        cols = slice(j * width + at, j * width + at + half)
        total[0:HALO, cols] = jnp.where(here == 0, 0.0, total[0:HALO, cols])
        return sum(
            taps[i, j : j + 1, at : at + half]
            * total[HALO - i : HALO - i + rows, cols].astype(BF16).astype(F32)
            for i in range(3)
        )

    def exchange(h, out, into, send, recv):
        @pl.loop(0, shards - 1)
        def _(n):
            to = lax.rem(here + 1 + n, shards)
            remote(out.at[h, to], into.at[h, here], send.at[h], recv.at[h], device(to)).start()

        into[h, here] = out[h, here]

    others = pl.ds(0, shards - 1)

    def arrivals(h, into, send, recv):
        remote(into.at[h, others], into.at[h, others], send.at[h], recv.at[h]).wait_recv()

    for h in range(2):
        for fz in pending:
            multiply(fz, False, (2 + h, 2, 2))
        signal = short(1, h * half) * short(2, h * half)
        stacked = jnp.concatenate([signal[:, :quarter], signal[:, quarter:]], axis=0)
        sig_out[h] = stacked.T.astype(BF16).reshape(shards, 2, 2 * rows)
        exchange(h, sig_out, sig_all, sig_send, sig_recv)
    for fz in pending:
        multiply(fz, False, (0, 1, 2))
    for at in (0, half):
        query[:, at : at + half] = short(0, at)

    lines = 2 * shards
    blocks_of = (slice(0, rows), slice(rows, 2 * rows))
    mul = functools.partial(jnp.dot, preferred_element_type=F32)
    back = lambda a, b: lax.dot_general(a, b, (((0,), (0,)), ((), ())), preferred_element_type=F32)
    join = functools.partial(jnp.concatenate, axis=0)

    def split(value):
        high = value.astype(BF16)
        return high, (value - high.astype(F32)).astype(BF16)

    def within(real, imag):
        high, low = split(join([real, imag]))
        cos = mul(high, inner[0]) + mul(low, inner[0]) + mul(high, inner[1])
        sin = mul(high, inner[2]) + mul(low, inner[2]) + mul(high, inner[3])
        return cos[: 2 * lines], cos[2 * lines :], sin[: 2 * lines], sin[2 * lines :]

    def convolve(h):
        data = [sig_all[h, :, :, u].reshape(lines, rows) for u in blocks_of]
        data = [mul(across[0], d) + mul(across[1], d) for d in data]
        real, imag = join([d[:lines] for d in data]), join([d[lines:] for d in data])
        cos, sin = turns[0], turns[1]
        real_cos, imag_cos, real_sin, imag_sin = within(
            real * cos + imag * sin, imag * cos - real * sin
        )
        real, imag = real_cos + imag_sin, imag_cos - real_sin
        freq_real, freq_imag = freq_wide[h, 0], freq_wide[h, 1]
        real_cos, imag_cos, real_sin, imag_sin = within(
            real * freq_real - imag * freq_imag, real * freq_imag + imag * freq_real
        )
        real, imag = real_cos - imag_sin, imag_cos + real_sin
        real, imag = real * cos - imag * sin, imag * cos + real * sin
        for n, u in enumerate(blocks_of):
            own = slice(n * lines, (n + 1) * lines)
            high, low = split(join([real[own], imag[own]]))
            data = back(across[0], high) + back(across[0], low) + back(across[1], high)
            data = (data * (1 / (shards * rows))).astype(BF16)
            conv_out[h, :, :, u] = data.reshape(shards, 2, rows)
        exchange(h, conv_out, conv_all, conv_send, conv_recv)

    for d in range(1, xs):
        of = lax.rem(x + xs - d, xs)
        theirs = grad_all.at[:, pl.ds(pl.multiple_of(share * of, share), share)]
        remote(theirs, theirs, grad_x_send.at[d - 1], grad_x_recv.at[d - 1]).wait_recv()
    grad_turned[...] = grad_all[...].reshape(near * rows, blocks * 128).T
    remote(freq_all.at[others], freq_all.at[others], freq_send, freq_recv).wait_recv()
    for h in range(2):
        for p in range(2):
            freq_wide[h, p] = join(
                [freq_all[:, h, p, :, u].reshape(lines, rows).astype(F32) for u in blocks_of]
            )
    for h in range(2):
        arrivals(h, sig_all, sig_send, sig_recv)
        convolve(h)

    def gated_from(h, fy, of_core):
        return gated_all.at[h, wrap(y - turn * fy, ys) * 2 + of_core]

    def pass_gated(h, fy, step):
        block = gated_from(h, fy, core)
        sem = (h, y_low + (ys // 2 if 2 * abs(fy + step) == ys else fy + step))
        start(remote(block, block, gated_send.at[sem], gated_recv.at[sem], by_axis("y", step)))

    def pair_gated(h, fy):
        block, sem = gated_from(h, fy, core), (h, y_low + fy)
        start(remote(block, block, pair_send.at[sem], pair_recv.at[sem], twin))

    def take_gated(h, fy):
        block, sem = gated_from(h, fy, core), (h, y_low + fy)
        remote(block, block, gated_send.at[sem], gated_recv.at[sem]).wait_recv()
        if abs(fy) == 1 and fy == 1 - 2 * h:
            pass_gated(h, fy, fy)
        pair_gated(h, fy)

    def gate(h):
        arrivals(h, conv_all, conv_send, conv_recv)
        conv = conv_all[h].reshape(lines, 2 * rows).astype(F32).T
        for n in range(2):
            at = h * half + n * quarter
            value = query[:, at : at + quarter] * conv[n * rows : (n + 1) * rows]
            gated_all[h, group, :, n * quarter : (n + 1) * quarter] = value.astype(BF16)
        pass_gated(h, 0, 1)
        pass_gated(h, 0, -1)
        pair_gated(h, 0)
        gated[:, h * half : (h + 1) * half] = gated_all[h, group]

    count = w_grad.shape[0]

    def distance(h, k):
        return lax.rem((1 - 2 * h) * (z - core * blocks - k) + 2 * zs, zs)

    def relay_copy(h, k, to, n):
        step = z - (1 - 2 * h) * to
        return remote(
            part_out.at[h, k], relayed.at[h, n], relay_send.at[h, k], relay_recv.at[h, n],
            {"z": wrap(step, zs), "y": y, "core": core, "ch": x},
        )

    def final_copy(h, k, c, n):
        return remote(
            part_out.at[h, k, pl.ds(c * count, count)], part_all.at[h, n],
            part_send.at[h, k, c], part_recv.at[h],
            {"z": core * blocks + k, "y": y, "core": c, "ch": x},
        )

    ends = {0: 0, 1: 1, zs - 1: 2, 2: 3, zs - 2: 4}
    relays = {3: (1, 0), 4: (2, 1), zs - 3: (-1, 2)}

    def send_part(h, k, away, act):
        for c in range(2):
            if away:
                act(final_copy(h, k, c, ends[away]))
            else:

                @pl.when(core != c)
                def _():
                    act(final_copy(h, k, c, 0))

    def products(h):
        for fy in range(-y_low, ys // 2 + 1):
            block, sem = gated_from(h, fy, 1 - core), (h, y_low + mirror(fy, ys))
            remote(block, block, pair_send.at[sem], pair_recv.at[sem]).wait_recv()
        right = gated_all[h].reshape(near * rows, half)
        for k in range(blocks):
            part_out[h, k] = mul(grad_turned[128 * k : 128 * (k + 1)], right).astype(BF16)
            for away, (to, n) in relays.items():

                @pl.when(distance(h, k) == away)
                def _():
                    relay_copy(h, k, to, n).start()

            for away in (1, zs - 1, 0):

                @pl.when(distance(h, k) == away)
                def _():
                    send_part(h, k, away, lambda copy: copy.start())
                    if not away:
                        part_all[h, 0] = part_out[h, k, pl.ds(pl.multiple_of(core * count, count), count)]

    def combine(h):
        for k in range(blocks):
            for away, inputs in ((2, (0, 1)), (zs - 2, (2,))):

                @pl.when(distance(h, k) == away)
                def _():
                    for n in inputs:
                        remote(
                            relayed.at[h, n], relayed.at[h, n], relay_send.at[h, k], relay_recv.at[h, n]
                        ).wait_recv()
                    total_part = part_out[h, k].astype(F32)
                    for n in inputs:
                        total_part += relayed[h, n].astype(F32)
                    part_out[h, k] = total_part.astype(BF16)
                    send_part(h, k, away, lambda copy: copy.start())

    gate(0)
    gate(1)
    take_gated(0, 1)
    take_gated(1, -1)
    take_gated(0, -1)
    take_gated(1, 1)
    take_gated(0, 2)
    products(0)
    take_gated(1, 2)
    products(1)
    combine(0)
    combine(1)
    keeps = core == z // blocks

    def close_parts(h, number):
        some = part_all.at[h, pl.ds(0, number)]
        remote(some, some, part_send.at[h, 0, 0], part_recv.at[h]).wait_recv()

    for h in range(2):

        @pl.when(keeps)
        def _():
            close_parts(h, len(ends) - 1)

        @pl.when(jnp.logical_not(keeps))
        def _():
            close_parts(h, len(ends))

        w_grad[:, h * half : (h + 1) * half] = sum(part_all[h, n].astype(F32) for n in range(len(ends)))
        for k in range(blocks):
            for away in range(zs):

                @pl.when(distance(h, k) == away)
                def _():
                    if away in relays:
                        relay_copy(h, k, *relays[away]).wait_send()
                    else:
                        send_part(h, k, away, lambda copy: copy.wait_send())

    for copy in sends:
        copy.wait_send()
    remote(grad_arrivals, grad_arrivals, grad_send, grad_recv).wait_send()
    remote(freq_all.at[others], freq_all.at[others], freq_send, freq_recv).wait_send()
    for h in range(2):
        for into, send, recv in ((sig_all, sig_send, sig_recv), (conv_all, conv_send, conv_recv)):
            remote(into.at[h, others], into.at[h, others], send.at[h], recv.at[h]).wait_send()


def settle_kernel(a, b, a_out, b_out):
    a_out[...] = a[...]
    b_out[...] = b[...]


def on_device(features, w_in, short_filter, filter_spectrum, out_grad):
    zs, ys, xs = sizes = tuple(lax.axis_size(a) for a in ("z", "y", "ch"))
    rows, depth = features.shape
    piece, _, width = w_in.shape
    flat = 3 * width
    half = width // 2
    shards, near = zs * ys * 2, ys * 2
    per = half // shards // 2
    message = (2, shards, per, 2 * rows)
    count = out_grad.shape[1] // shards
    dma = pltpu.SemaphoreType.DMA
    vmem = pl.BlockSpec(memory_space=pltpu.VMEM)
    hbm = pl.BlockSpec(memory_space=pl.ANY)
    fixed = [jnp.asarray(t) for t in tables(shards, rows, per)]
    outs = (
        jax.ShapeDtypeStruct((rows, width), BF16),
        jax.ShapeDtypeStruct((count, width), F32),
    )
    results = pl.pallas_call(
        functools.partial(operator_kernel, sizes),
        out_shape=outs,
        in_specs=[hbm] * 8,
        out_specs=(vmem, vmem),
        scratch_shapes=[
            pltpu.VMEM((rows + HALO, depth * xs), BF16),
            pltpu.VMEM((piece * shards, flat), BF16),
            pltpu.VMEM((rows + HALO, flat), F32),
            pltpu.VMEM((rows, width), F32),
            pltpu.VMEM((2, rows, width), F32),
            pltpu.VMEM((shards, 2, 2, per, 2 * rows), BF16),
            pltpu.VMEM((shards, 2, 2, per, 2 * rows), BF16),
            pltpu.VMEM((2, 2, 2 * per * shards, rows), F32),
            pltpu.VMEM((near, rows, zs // 2 * 128), BF16),
            pltpu.VMEM((zs // 2 * 128, near * rows), BF16),
            *[pltpu.VMEM(message, BF16)] * 4,
            pltpu.VMEM((2, near, rows, half), BF16),
            pltpu.VMEM((2, zs // 2, 2 * count, half), BF16),
            pltpu.VMEM((2, 5, count, half), BF16),
            pltpu.VMEM((2, 3, 2 * count, half), BF16),
            *[pltpu.VMEM(t.shape, t.dtype) for t in fixed],
            pltpu.VMEM(short_filter.shape, F32),
            dma((9 + zs // 2,)), dma((2, zs, ys)), dma((2, zs, ys)), dma((zs, ys)), dma((zs, ys)),
            dma((xs - 1,)), dma((xs - 1,)), dma((xs - 1,)), dma((xs - 1,)), dma, dma, dma, dma,
            dma, dma, dma((xs - 1,)), dma((xs - 1,)), dma((2,)), dma((2,)),
            dma((2,)), dma((2,)), dma((2, ys)), dma((2, ys)), dma((2, ys)), dma((2, ys)), dma((2, zs // 2, 2)), dma((2,)),
            dma((2, zs // 2)), dma((2, 3)),
        ],
        compiler_params=pltpu.CompilerParams(
            collective_id=0, has_side_effects=True, vmem_limit_bytes=56 << 20
        ),
        name="operator",
    )(features, w_in.transpose(1, 0, 2), short_filter, filter_spectrum, out_grad, *fixed)
    return pl.pallas_call(
        settle_kernel, out_shape=outs, in_specs=[vmem] * 2, out_specs=(vmem, vmem), name="settle"
    )(*results)


def solution(mesh):
    fine = Mesh(mesh.devices.reshape(8, 4, 2, 4), ("z", "y", "core", "ch"))
    in_specs = (
        P(CTX, "ch"),
        P(CTX, None, "ch"),
        P(None, None, "ch"),
        P(None, CTX, "ch"),
        P(CTX, None),
    )
    out_specs = (P(CTX, "ch"), P(CTX, "ch"))
    return jax.shard_map(
        on_device, mesh=fine, in_specs=in_specs, out_specs=out_specs, check_vma=False
    )
```
